128 devices in a mesh: region: 16 (over z, y), survey: 8 (over x, core).
Axes of the slice: x: 4, y: 4, z: 4, core: 2. Of those that a mesh axis runs over, the one named last changes fastest.
Arguments:
- sensitivity: bfloat16 [512, 512, 4096], P(('region', 'survey')), may hold values from -0.09375 to 0.09375
- observed: float32 [512, 8, 512], P(('region', 'survey')), may hold values from -6 to 6
- data_weight: float32 [512, 512], P(('region', 'survey')), may hold values from 0.5 to 2
- data_counts: int32 [512], P(('region', 'survey')), may hold values from 128 to 512
- tile_bricks: int32 [512, 32], P(('region', 'survey')), may hold values from 0 to 65535, as said below
- start_model: float32 [256, 256, 8, 128], P('region', 'survey'), may hold values from -6 to 6
- active_cells: int32 [256, 256, 128], P('region', 'survey'), may hold values from 0 to 1
- face_links: int32 [256, 256, 128], P('region', 'survey'), may hold values from 0 to 63, as said below
- reg_weight: float32 [8], replicated, may hold values from 0.3 to 3
Outputs:
- final_model: float32 [256, 256, 8, 128], P('region', 'survey')
- misfit: float32 [512, 8, 512], P(('region', 'survey'))
The draws below stay inside these ranges and needn't reach their ends.
Inputs may be any that keep to these rules, and one draw needn't show every extreme that they name: `tile_bricks`: brick b lies on owning device b // 512 (region index times 8 plus survey index), at its slab's layer (b % 512) // 32 and row b % 32. The 128 entries of one device's tiles name bricks of at most 2 per owning device; one owning device, the same for all, is named exactly 2 times by every device's tiles. Entries may repeat. `face_links`: bit k (value 2^k) is 1 exactly when the cell and its neighbour n_k are both active, with k ordered as in the reference program.
All inputs are finite; a program needn't handle non-finite values.
Results may differ from the reference program's by a relative error of at most 0.0031.
Values may be sent and summed in bfloat16 or wider, within the bound.
A program may use at most 128 MiB of HBM per device.

```python
import math
import jax
import jax.numpy as jnp
from jax import lax

ZS = 16
NYD = 32
NX = 128
NBT = 32
ND = 512
SAMPLES = 8
TILE_DEV = 4
ITERS = 2
SLABS = 16
STRIPS = 8
OWNERS = 128
CAP = 2
NZ = 256
NY = 256
BRICKS = 65536
TILES = 512


def draw_tile_bricks(key, part):
    slots = OWNERS * CAP
    requests = TILE_DEV * NBT
    hot_owner = jax.random.randint(jax.random.fold_in(key, 11), (), 0, OWNERS)
    slot_owner = jnp.arange(slots, dtype=jnp.int32) // CAP
    shallow = (SLABS - 1 - slot_owner // STRIPS) * 128
    forced = jnp.where(slot_owner == hot_owner, 1 << 20, 0)
    raw_scores = jax.random.randint(jax.random.fold_in(key, 12), (OWNERS, slots), 0, 4096)
    scores = (raw_scores + shallow[None, :] + forced[None, :]) * slots + jnp.arange(slots, dtype=jnp.int32)[None, :]
    chosen = lax.top_k(scores, requests)[1].astype(jnp.int32)
    order_keys = jax.random.split(jax.random.fold_in(key, 13), OWNERS)

    def shuffle_row(row_key, chosen_row):
        return chosen_row[jax.random.permutation(row_key, requests)]
    shuffled = jax.vmap(shuffle_row)(order_keys, chosen)
    owner_ids = shuffled // CAP
    local_ids = jax.random.randint(jax.random.fold_in(key, 14), (OWNERS, requests), 0, ZS * NYD)
    brick_ids = owner_ids * (ZS * NYD) + local_ids
    return brick_ids.reshape(TILES, NBT).astype(jnp.int32)


def cell_layout(key):
    surface = jax.random.randint(jax.random.fold_in(key, 21), (NY, NX), 0, 4)
    layers = jnp.arange(NZ, dtype=jnp.int32)[:, None, None]
    holes = jax.random.randint(jax.random.fold_in(key, 22), (NZ, NY, NX), 0, 16)
    return ((layers >= surface[None, :, :]) & (holes > 0)).astype(jnp.int32)


def draw_active_cells(key, part):
    return cell_layout(key)


def draw_face_links(key, part):
    live = cell_layout(key)
    padded = jnp.pad(live, 1)
    centre = padded[1:-1, 1:-1, 1:-1]
    neighbours = [padded[:-2, 1:-1, 1:-1], padded[2:, 1:-1, 1:-1], padded[1:-1, :-2, 1:-1], padded[1:-1, 2:, 1:-1], padded[1:-1, 1:-1, :-2], padded[1:-1, 1:-1, 2:]]
    coded = jnp.zeros_like(centre)
    for number in range(6):
        coded = coded + centre * neighbours[number] * 2 ** number
    return coded.astype(jnp.int32)


def set_ends(entries, key, low, largest):
    dims = entries.shape
    place = [jax.random.randint(jax.random.fold_in(key, axis), (), 0, dims[axis]) for axis in range(len(dims))]
    entries = entries.at[tuple(place)].set(low)
    longest = dims.index(max(dims))
    place[longest] = (place[longest] + 1) % dims[longest]
    return entries.at[tuple(place)].set(largest)


def block_scale(rng, shape, shards, least, largest):
    def one(position, parts):
        steps = jax.random.uniform(jax.random.fold_in(jax.random.fold_in(rng, 6), position), (parts,), jnp.float32, least / len(shards), largest / len(shards))
        return jnp.repeat(jnp.exp(steps), shape[position] // parts).reshape((-1,) + (1,) * (len(shape) - position - 1))

    loudness = one(*shards[0])
    for cut in shards[1:]:
        loudness = loudness * one(*cut)
    return loudness


def bell_draw(rng, shape, scale, most, shards=(), kind=jnp.bfloat16):
    drawn = jax.random.normal(rng, shape, jnp.float32) * scale
    if len(shards) > 0:
        drawn = block_scale(rng, shape, shards, -0.22, 0.18) * drawn
    return jnp.clip(drawn, min=-most, max=most).astype(kind)


def setup_inputs(seed: int = 0) -> dict:
    keys = jax.random.split(jax.random.key(seed), 10)
    return {
        "sensitivity": bell_draw(keys[0], (TILES, ND, NBT * NX), (NBT * NX) ** -0.5, 0.09375, ((0, 128),)),
        "observed": bell_draw(keys[1], (TILES, SAMPLES, ND), 1.0, 6.0, ((0, 128),), jnp.float32),
        "data_weight": jnp.clip(jnp.exp(math.log(2.0) - 1.3862944 * jax.random.uniform(keys[2], (TILES, ND), jnp.float32) ** block_scale(keys[2], (TILES, ND), ((0, 128),), -0.2, 0.2)), 0.5, 2.0),
        "data_counts": set_ends(jax.random.randint(keys[3], (TILES,), ND // 4, ND + 1), jax.random.fold_in(keys[3], 1), ND // 4, ND).astype(jnp.int32),
        "tile_bricks": draw_tile_bricks(jax.random.fold_in(keys[9], 71), 0),
        "start_model": bell_draw(keys[5], (NZ, NY, SAMPLES, NX), 1.0, 6.0, ((0, 16), (1, 8)), jnp.float32),
        "active_cells": draw_active_cells(jax.random.fold_in(keys[9], 71), 0),
        "face_links": draw_face_links(jax.random.fold_in(keys[9], 71), 0),
        "reg_weight": jnp.clip(jnp.exp(jax.random.uniform(keys[8], (SAMPLES,), jnp.float32, math.log(0.3), math.log(3.0))), 0.3, 3.0),
    }


EPS_SQ = 0.09

def stencil_list(padded):
    centre = padded[1:-1, 1:-1]
    zero_rim = jnp.zeros_like(centre[..., :1])
    neighbours = [padded[:-2, 1:-1], padded[2:, 1:-1], padded[1:-1, :-2], padded[1:-1, 2:], jnp.concatenate([zero_rim, centre[..., :-1]], axis=3), jnp.concatenate([centre[..., 1:], zero_rim], axis=3)]
    return (centre, neighbours)

def irls_weights(centre, neighbours, link_bits, depth_index, active, depth_count):
    smallness = active * (1.0 + 2.0 * depth_index / depth_count) / jnp.sqrt(centre * centre + EPS_SQ)
    offsets = [-1.0, 1.0, 0.0, 0.0, 0.0, 0.0]
    face_weights = []
    for number in range(6):
        depth_level = 1.0 + (2.0 * depth_index + offsets[number]) / depth_count
        difference = centre - neighbours[number]
        face_weights.append(link_bits[number] * depth_level / jnp.sqrt(difference * difference + EPS_SQ))
    return (smallness, face_weights)

def reg_gradient(centre, neighbours, smallness, face_weights):
    running = smallness * centre
    for number in range(6):
        running = running + face_weights[number] * (centre - neighbours[number])
    return running

def reg_curvature(centre, neighbours, smallness, face_weights):
    running = smallness * centre * centre
    for number in range(6):
        difference = centre - neighbours[number]
        running = running + 0.5 * face_weights[number] * difference * difference
    return lax.optimization_barrier(jnp.sum(running, axis=(0, 1, 3)))

def to_bricks(field):
    shaped = field.reshape(SLABS, ZS, STRIPS, NYD, SAMPLES, NX)
    return shaped.transpose(0, 2, 1, 3, 4, 5).reshape(BRICKS, SAMPLES, NX)

def from_bricks(flattened):
    shaped = flattened.reshape(SLABS, STRIPS, ZS, NYD, SAMPLES, NX)
    return shaped.transpose(0, 2, 1, 3, 4, 5).reshape(NZ, NY, SAMPLES, NX)

def forward(field, sensitivity, tile_bricks):
    lowered = lax.optimization_barrier(field.astype(jnp.bfloat16))
    brick_store = to_bricks(lowered)

    def per_tile(operands):
        sensor, brick_ids = operands
        picked = brick_store[brick_ids].astype(jnp.float32)
        sensor_view = sensor.reshape(ND, NBT, NX).astype(jnp.float32)
        return jnp.einsum('dbx,bsx->sd', sensor_view, picked, precision=lax.Precision.HIGHEST)
    return lax.map(per_tile, (sensitivity, tile_bricks))

def backward(weighted, sensitivity, tile_bricks):

    def per_tile(operands):
        sensor, weights_low = operands
        sensor_view = sensor.reshape(ND, NBT, NX).astype(jnp.float32)
        return jnp.einsum('sd,dbx->bsx', weights_low.astype(jnp.float32), sensor_view, precision=lax.Precision.HIGHEST)
    products = lax.map(per_tile, (sensitivity, weighted))
    flattened = jnp.zeros((BRICKS, SAMPLES, NX), jnp.float32)
    flattened = flattened.at[tile_bricks.reshape(-1)].add(products.reshape(-1, SAMPLES, NX))
    return from_bricks(flattened)

def pad_cells(field):
    return jnp.pad(field, ((1, 1), (1, 1), (0, 0), (0, 0)))

def reference(sensitivity, observed, data_weight, data_counts, tile_bricks, start_model, active_cells, face_links, reg_weight):
    active = active_cells.astype(jnp.float32)[:, :, None, :]
    link_bits = [(face_links // 2 ** number % 2).astype(jnp.float32)[:, :, None, :] for number in range(6)]
    depth_index = jnp.arange(NZ, dtype=jnp.float32).reshape(NZ, 1, 1, 1)
    row_mask = (jnp.arange(ND, dtype=jnp.int32)[None, None, :] < data_counts[:, None, None]).astype(jnp.float32)
    weight_sq = row_mask * (data_weight * data_weight)[:, None, :]
    reg_scale = reg_weight[None, None, :, None]
    model_now = start_model * active
    predicted = forward(model_now, sensitivity, tile_bricks)
    for iteration in range(ITERS):
        weighted = (weight_sq * (predicted - observed)).astype(jnp.bfloat16)
        data_grad = backward(weighted, sensitivity, tile_bricks)
        centre, neighbours = stencil_list(pad_cells(model_now))
        smallness, face_weights = irls_weights(centre, neighbours, link_bits, depth_index, active, NZ)
        gradient = active * data_grad + reg_scale * reg_gradient(centre, neighbours, smallness, face_weights)
        step_pred = forward(gradient, sensitivity, tile_bricks)
        grad_centre, grad_neighbours = stencil_list(pad_cells(gradient))
        reg_curv = reg_curvature(grad_centre, grad_neighbours, smallness, face_weights)
        grad_norm = lax.optimization_barrier(jnp.sum(gradient * gradient, axis=(0, 1, 3)))
        data_curv = lax.optimization_barrier(jnp.sum(weight_sq * step_pred * step_pred, axis=(0, 2)))
        step_length = grad_norm / (data_curv + reg_weight * reg_curv)
        model_now = model_now - step_length[None, None, :, None] * gradient
        predicted = predicted - step_length[None, :, None] * step_pred
    misfit = row_mask * data_weight[:, None, :] * (predicted - observed)
    return (model_now, misfit)
```

```python
import functools

import jax
import jax.numpy as jnp
from jax import lax
from jax.experimental import pallas as pl
from jax.experimental.pallas import tpu as pltpu
from jax.sharding import PartitionSpec as P

MESH = pl.DeviceIdType.MESH
EPS_SQ = 0.09
F32, BF16 = jnp.float32, jnp.bfloat16


def kernel(
    dims,
    slot_of,
    entry_of,
    counts,
    reg_weight,
    ask,
    observed,
    data_weight,
    active,
    links,
    model_hbm,
    sens_hbm,
    model_out,
    grad_out,
    step_out,
    misfit_out,
    sens,
    model,
    grad,
    data_grad,
    sums,
    reg_part,
    w_small,
    w_z,
    w_y,
    w_x,
    low_z,
    asked,
    asked_s,
    picked,
    product,
    predicted,
    residual,
    step_pred,
    sent1,
    sent2,
    sent3,
    sent4,
    sent5,
    came1,
    came2,
    came3,
    came4,
    came5,
    spread,
    one_hot,
    stage_y,
    halo_z,
    halo_y,
    grad_z,
    grad_y,
    sum_mine,
    sum_a,
    sum_b,
    load_sem,
    send_sem,
    recv_sem,
):
    regions, surveys, layers, rows, tiles, width, slots = dims
    owners = regions * surveys
    cells = layers * rows
    depth_count = float(layers * regions)
    region, survey = lax.axis_index("region"), lax.axis_index("survey")
    me = region * surveys + survey

    def device(flat):
        return (flat // surveys, flat % surveys)

    sent = (None, sent1, sent2, sent3, sent4, sent5)
    came = (None, came1, came2, came3, came4, came5)
    barrier = pltpu.get_barrier_semaphore()

    def greet(i, c):
        pl.semaphore_signal(
            barrier, inc=1, device_id=device((me + i) % owners), device_id_type=MESH
        )
        return c

    lax.fori_loop(1, owners, greet, 0)
    load_model = pltpu.make_async_copy(model_hbm, model, load_sem.at[0])
    load_model.start()
    load_sens = pltpu.make_async_copy(sens_hbm, sens, load_sem.at[1])
    load_sens.start()
    pl.semaphore_wait(barrier, owners - 1)

    def remote(src, dst, number, to):
        return pltpu.make_async_remote_copy(
            src_ref=src,
            dst_ref=dst,
            send_sem=send_sem.at[number],
            recv_sem=recv_sem.at[number],
            device_id=to,
            device_id_type=MESH,
        )

    def await_bytes(ref, sem):
        pltpu.make_async_copy(ref, ref, sem).wait()

    def send_ids(i, c):
        to = (me + i) % owners
        remote(ask.at[to], asked.at[me], 0, device(to)).start()
        return c

    lax.fori_loop(1, owners, send_ids, 0)
    asked[me] = ask[me]

    load_model.wait()

    def row_of(ref, b):
        return jnp.broadcast_to(ref[pl.ds(b, 1), :], (8, 128))

    def mask_model(b, c):
        model[b] = model[b] * row_of(active, b).astype(F32)
        return c

    lax.fori_loop(0, cells, mask_model, 0, unroll=8)

    up_z = ((region + 1) % regions, survey)
    down_z = ((region + regions - 1) % regions, survey)
    up_y = (region, (survey + 1) % surveys)
    down_y = (region, (survey + surveys - 1) % surveys)

    def send_halo(field, into_z, into_y, base, stage):
        for z in range(layers):
            stage_y[stage, 0, z] = field[z * rows]
            stage_y[stage, 1, z] = field[z * rows + rows - 1]
        last = (layers - 1) * rows
        remote(field.at[pl.ds(0, rows)], into_z.at[1], base, down_z).start()
        remote(field.at[pl.ds(last, rows)], into_z.at[0], base + 1, up_z).start()
        remote(stage_y.at[stage, 0], into_y.at[1], base + 2, down_y).start()
        remote(stage_y.at[stage, 1], into_y.at[0], base + 3, up_y).start()

    def await_halo(into_z, into_y, base):
        await_bytes(into_z.at[1], recv_sem.at[base])
        await_bytes(into_z.at[0], recv_sem.at[base + 1])
        await_bytes(into_y.at[1], recv_sem.at[base + 2])
        await_bytes(into_y.at[0], recv_sem.at[base + 3])

    def sent_halo(field, base, stage):
        await_bytes(field.at[pl.ds(0, rows)], send_sem.at[base])
        await_bytes(field.at[pl.ds(0, rows)], send_sem.at[base + 1])
        await_bytes(stage_y.at[stage, 0], send_sem.at[base + 2])
        await_bytes(stage_y.at[stage, 1], send_sem.at[base + 3])

    send_halo(model, halo_z, halo_y, 10, 0)

    await_bytes(asked.at[pl.ds(0, owners - 1)], recv_sem.at[0])
    to_scalar = pltpu.make_async_copy(asked, asked_s, load_sem.at[2])
    to_scalar.start()
    to_scalar.wait()

    def exchange(number, first_of, second_of):
        def send(i, c):
            to = (me + i) % owners
            sent[number][2 * to] = first_of(to)
            sent[number][2 * to + 1] = second_of(to)
            two = pl.ds(2 * to, 2)
            remote(
                sent[number].at[two], came[number].at[pl.ds(2 * me, 2)], number, device(to)
            ).start()
            return c

        lax.fori_loop(1, owners, send, 0)
        came[number][2 * me] = first_of(me)
        came[number][2 * me + 1] = second_of(me)

    def fetch(field, number):
        exchange(
            number,
            lambda to: field[asked_s[to, 0, 0]].astype(BF16),
            lambda to: field[asked_s[to, 0, 1]].astype(BF16),
        )

    def give_back(number):
        exchange(
            number,
            lambda to: product[entry_of[2 * to]].astype(BF16),
            lambda to: product[entry_of[2 * to + 1]].astype(BF16),
        )

    def await_round(number):
        await_bytes(came[number].at[pl.ds(0, 2 * owners - 2)], recv_sem.at[number])

    fetch(model, 1)

    ids = jnp.transpose(asked[:, 0, :].astype(F32))
    numbers = lax.broadcasted_iota(jnp.int32, (cells, owners), 0).astype(F32)
    for rank in range(2):
        named = jnp.broadcast_to(ids[2 + rank : 3 + rank, :], (cells, owners))
        one_hot[:, rank * owners : (rank + 1) * owners] = jnp.where(
            numbers == named, 1.0, 0.0
        ).astype(BF16)

    lane = lax.broadcasted_iota(jnp.int32, (8, 128), 1)
    sample = lax.broadcasted_iota(jnp.int32, (8, 128), 0)
    scale = jnp.zeros((8, 128), F32)
    for s in range(8):
        scale = jnp.where(sample == s, reg_weight[s], scale)

    def bit(word, k):
        return ((word // 2**k) % 2).astype(F32)

    def regularize():
        def flux(difference, link):
            weight = link * lax.rsqrt(difference * difference + EPS_SQ)
            return weight, weight * difference

        z_base = (region * layers).astype(F32)
        for y in range(rows):
            link = bit(row_of(links, y), 0) * (1.0 + (2.0 * z_base - 1.0) / depth_count)
            low_z[y] = flux(model[y] - halo_z[0, y], link)[1]

        def one_layer(z, c, last):
            depth = z_base + (z if last else z.astype(F32))
            h_here = 1.0 + 2.0 * depth / depth_count
            h_next = 1.0 + (2.0 * depth + 1.0) / depth_count
            first = model[z * rows]
            _, before = flux(
                first - halo_y[0, z], bit(row_of(links, z * rows), 2) * h_here
            )
            for y in range(rows):
                b = z * rows + y
                here = model[b]
                if last:
                    above = halo_z[1, y]
                else:
                    above = model[b + rows]
                beside = model[b + 1] if y < rows - 1 else halo_y[1, z]
                word = row_of(links, b)
                small = (
                    row_of(active, b).astype(F32) * h_here * lax.rsqrt(here * here + EPS_SQ)
                )
                wz, fz = flux(above - here, bit(word, 1) * h_next)
                wy, fy = flux(beside - here, bit(word, 3) * h_here)
                wx, fx = flux(pltpu.roll(here, 127, 1) - here, bit(word, 5) * h_here)
                total = (
                    small * here
                    + (low_z[y] - fz)
                    + (before - fy)
                    + (pltpu.roll(fx, 1, 1) - fx)
                )
                reg_part[b] = scale * total
                w_small[b] = small
                w_z[b] = wz
                w_y[b] = wy
                w_x[b] = wx
                low_z[y] = fz
                before = fy
            return c

        lax.fori_loop(0, layers - 1, functools.partial(one_layer, last=False), 0)
        one_layer(layers - 1, 0, True)

    def curvature(after):
        def one_layer(z, carry, last):
            norm, curv = carry
            for y in range(rows):
                b = z * rows + y
                here = grad[b]
                if last:
                    above = grad_z[after, y]
                else:
                    above = grad[b + rows]
                beside = grad[b + 1] if y < rows - 1 else grad_y[after, z]
                dz, dy, dx = above - here, beside - here, pltpu.roll(here, 127, 1) - here
                square = here * here
                norm = norm + square
                curv = curv + (
                    (w_small[b] * square + w_z[b] * (dz * dz))
                    + (w_y[b] * (dy * dy) + w_x[b] * (dx * dx))
                )
            return norm, curv

        zero = jnp.zeros((8, 128), F32)
        carry = lax.fori_loop(
            0, layers - 1, functools.partial(one_layer, last=False), (zero, zero)
        )
        norm, curv = one_layer(layers - 1, carry, True)
        return (
            jnp.sum(norm, axis=1, keepdims=True),
            jnp.sum(curv * scale, axis=1, keepdims=True),
        )

    def pick(number):
        def one(e, c):
            t, column = e // width, e % width
            at = pl.ds(pl.multiple_of(column * 128, 128), 128)
            picked[t, :, at] = came[number][slot_of[e]].astype(F32)
            return c

        lax.fori_loop(0, tiles * width, one, 0, unroll=4)

    def forward(t):
        chunk = 1024
        total = jnp.zeros((8, slots), F32)
        for c in range(width * 128 // chunk):
            at = slice(c * chunk, (c + 1) * chunk)
            total = total + lax.dot_general(
                picked[t, :, at].astype(BF16),
                sens[t, :, at],
                (((1,), (1,)), ((), ())),
                preferred_element_type=F32,
            )
        return total

    def backward(t, weighted):
        chunk = 1024
        for c in range(width * 128 // chunk):
            made = lax.dot_general(
                weighted,
                sens[t, :, c * chunk : (c + 1) * chunk],
                (((1,), (0,)), ((), ())),
                preferred_element_type=F32,
            )
            for j in range(chunk // 128):
                entry = t * width + c * (chunk // 128) + j
                product[entry] = made[:, j * 128 : (j + 1) * 128]

    def mask_of(t):
        slot = lax.broadcasted_iota(jnp.int32, (1, slots), 1)
        return jnp.where(slot < counts[t], 1.0, 0.0)

    def weight_of(t):
        weight = data_weight[pl.ds(t, 1), :]
        return mask_of(t) * (weight * weight)

    def scatter(number):
        def widen(d, c):
            spread[pl.ds(pl.multiple_of(d * 8, 8), 8), :] = came[number][d].astype(F32)
            return c

        lax.fori_loop(0, 2 * owners, widen, 0, unroll=8)
        table = one_hot[...]
        for s in range(8):
            first = spread[pl.ds(s, owners, stride=16), :]
            second = spread[pl.ds(8 + s, owners, stride=16), :]
            blocks = jnp.concatenate([first, second], axis=0).astype(BF16)
            sums[pl.ds(s, cells, stride=8), :] = jnp.dot(
                table, blocks, preferred_element_type=F32
            )

    def make_gradient(step):
        def one(b, c):
            total = sums[pl.ds(pl.multiple_of(b * 8, 8), 8), :]
            if step is None:
                data_grad[b] = total
            else:
                total = data_grad[b] - step * total
            grad[b] = row_of(active, b).astype(F32) * total + reg_part[b]
            return c

        lax.fori_loop(0, cells, one, 0, unroll=8)

    def sum_start(mine, number):
        sum_mine[number, 0] = mine
        sum_a[number, survey] = mine

        def send(i, c):
            to = (survey + i) % surveys
            remote(
                sum_mine.at[number, 0], sum_a.at[number, survey], 6 + 2 * number, (region, to)
            ).start()
            return c

        lax.fori_loop(1, surveys, send, 0)

    def sum_end(number):
        await_bytes(sum_a.at[number, pl.ds(0, surveys - 1)], recv_sem.at[6 + 2 * number])
        part = sum_a[number, 0]
        for i in range(1, surveys):
            part = part + sum_a[number, i]
        sum_mine[number, 1] = part
        sum_b[number, region] = part

        def send(i, c):
            to = (region + i) % regions
            remote(
                sum_mine.at[number, 1], sum_b.at[number, region], 7 + 2 * number, (to, survey)
            ).start()
            return c

        lax.fori_loop(1, regions, send, 0)
        await_bytes(sum_b.at[number, pl.ds(0, regions - 1)], recv_sem.at[7 + 2 * number])
        whole = sum_b[number, 0]
        for i in range(1, regions):
            whole = whole + sum_b[number, i]
        norm = jnp.sum(jnp.where(lane == 0, whole, 0.0), axis=1, keepdims=True)
        curv = jnp.sum(jnp.where(lane == 1, whole, 0.0), axis=1, keepdims=True)
        return norm / curv

    def my_sums(norm, reg_curv, data_curv):
        return jnp.where(lane == 0, norm, jnp.where(lane == 1, reg_curv + data_curv, 0.0))

    await_halo(halo_z, halo_y, 10)
    regularize()
    load_sens.wait()

    await_round(1)
    pick(1)

    def first_pass(t, c):
        gap = forward(t) - observed[t]
        residual[t] = gap
        backward(t, (weight_of(t) * gap).astype(BF16))
        return c

    lax.fori_loop(0, tiles, first_pass, 0)
    give_back(2)
    await_round(2)
    scatter(2)
    make_gradient(None)
    fetch(grad, 3)
    send_halo(grad, grad_z, grad_y, 14, 1)
    await_halo(grad_z, grad_y, 14)
    norm, reg_curv = curvature(1)

    await_round(3)
    pick(3)

    def second_pass(t, total):
        made = forward(t)
        step_pred[t] = made
        scaled = weight_of(t) * made
        backward(t, scaled.astype(BF16))
        return total + jnp.sum(scaled * made, axis=1, keepdims=True)

    data_curv = lax.fori_loop(0, tiles, second_pass, jnp.zeros((8, 1), F32))
    sum_start(my_sums(norm, reg_curv, data_curv), 0)
    give_back(4)
    step = sum_end(0)
    sent_halo(model, 10, 0)
    sent_halo(grad, 14, 1)
    step_row = jnp.broadcast_to(step, (8, 128))

    def move(b, c):
        model[b] = model[b] - step_row * grad[b]
        return c

    lax.fori_loop(0, cells, move, 0, unroll=8)
    for side in range(2):
        for y in range(rows):
            halo_z[side, y] = halo_z[side, y] - step_row * grad_z[side, y]
        for z in range(layers):
            halo_y[side, z] = halo_y[side, z] - step_row * grad_y[side, z]
    save_model = pltpu.make_async_copy(model, model_out, load_sem.at[3])
    save_model.start()
    regularize()

    def move_gap(t, c):
        residual[t] = residual[t] - step * step_pred[t]
        return c

    lax.fori_loop(0, tiles, move_gap, 0)

    await_round(4)
    scatter(4)
    make_gradient(step_row)
    fetch(grad, 5)
    save_grad = pltpu.make_async_copy(grad, grad_out, load_sem.at[4])
    save_grad.start()
    for z in range(layers):
        stage_y[2, 0, z] = grad[z * rows]
    remote(grad.at[pl.ds(0, rows)], grad_z.at[2], 18, down_z).start()
    remote(stage_y.at[2, 0], grad_y.at[2], 19, down_y).start()
    await_bytes(grad_z.at[2], recv_sem.at[18])
    await_bytes(grad_y.at[2], recv_sem.at[19])
    norm, reg_curv = curvature(2)

    await_round(5)
    pick(5)

    def third_pass(t, total):
        made = forward(t)
        step_pred[t] = made
        return total + jnp.sum(weight_of(t) * made * made, axis=1, keepdims=True)

    data_curv = lax.fori_loop(0, tiles, third_pass, jnp.zeros((8, 1), F32))
    sum_start(my_sums(norm, reg_curv, data_curv), 1)
    step = sum_end(1)
    step_out[...] = jnp.broadcast_to(step, (8, 128))

    def finish(t, c):
        weight = mask_of(t) * data_weight[pl.ds(t, 1), :]
        misfit_out[t] = weight * (residual[t] - step * step_pred[t])
        return c

    lax.fori_loop(0, tiles, finish, 0)

    await_bytes(ask.at[pl.ds(0, owners - 1)], send_sem.at[0])
    for number in range(1, 6):
        await_bytes(sent[number].at[pl.ds(0, 2 * owners - 2)], send_sem.at[number])
    for number in range(2):
        await_bytes(sum_a.at[number, pl.ds(0, surveys - 1)], send_sem.at[6 + 2 * number])
        await_bytes(sum_b.at[number, pl.ds(0, regions - 1)], send_sem.at[7 + 2 * number])
    await_bytes(grad.at[pl.ds(0, rows)], send_sem.at[18])
    await_bytes(stage_y.at[2, 0], send_sem.at[19])
    save_model.wait()
    save_grad.wait()


def shards(
    regions,
    surveys,
    sensitivity,
    observed,
    data_weight,
    data_counts,
    tile_bricks,
    start_model,
    active_cells,
    face_links,
    reg_weight,
):
    layers, rows, samples, across = start_model.shape
    tiles, width = tile_bricks.shape
    slots = sensitivity.shape[1]
    owners, cells = regions * surveys, layers * rows
    entries = tiles * width

    wanted = tile_bricks.reshape(entries)
    owner_of, local_of = wanted // cells, wanted % cells
    number = jnp.arange(entries, dtype=jnp.int32)
    earlier = (owner_of[:, None] == owner_of[None, :]) & (number[None, :] < number[:, None])
    rank_of = jnp.sum(earlier.astype(jnp.int32), axis=1)
    slot_of = 2 * owner_of + rank_of
    hits = jnp.arange(2 * owners, dtype=jnp.int32)[:, None] == slot_of[None, :]
    ask = jnp.sum(jnp.where(hits, local_of[None, :] + 1, 0), axis=1) - 1
    entry_of = jnp.sum(jnp.where(hits, number[None, :], 0), axis=1)
    ask = ask.reshape(owners, 1, 2)
    ask = jnp.concatenate([jnp.maximum(ask, 0), ask], axis=2)
    ask = jnp.pad(ask, ((0, 0), (0, 0), (0, 124)))

    field = jax.ShapeDtypeStruct((cells, samples, across), F32)
    field_scratch = pltpu.VMEM(field.shape, F32)
    blocks = pltpu.VMEM((2 * owners, samples, across), BF16)
    data_scratch = pltpu.VMEM((tiles, samples, slots), F32)
    vmem = pl.BlockSpec(memory_space=pltpu.VMEM)
    smem = pl.BlockSpec(memory_space=pltpu.SMEM)
    anywhere = pl.BlockSpec(memory_space=pl.ANY)
    moved, gradient, step, misfit = pl.pallas_call(
        functools.partial(kernel, (regions, surveys, layers, rows, tiles, width, slots)),
        name="inversion",
        out_shape=(
            field,
            field,
            jax.ShapeDtypeStruct((samples, across), F32),
            jax.ShapeDtypeStruct((tiles, samples, slots), F32),
        ),
        in_specs=[smem] * 4 + [vmem] * 5 + [anywhere] * 2,
        out_specs=(anywhere, anywhere, vmem, vmem),
        scratch_shapes=[
            pltpu.VMEM(sensitivity.shape, BF16),
            field_scratch,
            field_scratch,
            field_scratch,
            pltpu.VMEM((cells * samples, across), F32),
            *[field_scratch] * 5,
            pltpu.VMEM((rows, 8, 128), F32),
            pltpu.VMEM((owners, 1, 128), jnp.int32),
            pltpu.SMEM((owners, 1, 128), jnp.int32),
            pltpu.VMEM((tiles, samples, width * 128), F32),
            pltpu.VMEM((entries, samples, across), F32),
            data_scratch,
            data_scratch,
            data_scratch,
            *[blocks] * 10,
            pltpu.VMEM((owners * 16, 128), F32),
            pltpu.VMEM((cells, 2 * owners), BF16),
            pltpu.VMEM((3, 2, layers, 8, 128), F32),
            pltpu.VMEM((2, rows, 8, 128), F32),
            pltpu.VMEM((2, layers, 8, 128), F32),
            pltpu.VMEM((3, rows, 8, 128), F32),
            pltpu.VMEM((3, layers, 8, 128), F32),
            pltpu.VMEM((2, 2, 8, 128), F32),
            pltpu.VMEM((2, surveys, 8, 128), F32),
            pltpu.VMEM((2, regions, 8, 128), F32),
            pltpu.SemaphoreType.DMA((5,)),
            pltpu.SemaphoreType.DMA((20,)),
            pltpu.SemaphoreType.DMA((20,)),
        ],
        compiler_params=pltpu.CompilerParams(
            collective_id=0, has_side_effects=True, vmem_limit_bytes=60 << 20
        ),
    )(
        slot_of,
        entry_of,
        data_counts,
        reg_weight,
        ask,
        observed,
        data_weight,
        active_cells.reshape(cells, across),
        face_links.reshape(cells, across),
        start_model.reshape(cells, samples, across),
        sensitivity,
    )
    final = moved.reshape(start_model.shape) - step * gradient.reshape(start_model.shape)
    return final, misfit


def solution(mesh):
    return jax.shard_map(
        functools.partial(shards, mesh.shape["region"], mesh.shape["survey"]),
        mesh=mesh,
        in_specs=(
            P(("region", "survey"), None, None),
            P(("region", "survey"), None, None),
            P(("region", "survey"), None),
            P(("region", "survey")),
            P(("region", "survey"), None),
            P("region", "survey", None, None),
            P("region", "survey", None),
            P("region", "survey", None),
            P(),
        ),
        out_specs=(P("region", "survey", None, None), P(("region", "survey"), None, None)),
        check_vma=False,
    )
```

```python
import functools

import jax
import jax.numpy as jnp
from jax import lax
from jax.experimental import pallas as pl
from jax.experimental.pallas import tpu as pltpu
from jax.sharding import PartitionSpec as P

MESH = pl.DeviceIdType.MESH
EPS_SQ = 0.09
F32, BF16 = jnp.float32, jnp.bfloat16


def kernel(
    dims,
    counts,
    reg_weight,
    bricks,
    observed_hbm,
    data_weight_hbm,
    active_hbm,
    links_hbm,
    model_hbm,
    sens_hbm,
    model_out,
    grad_out,
    step_out,
    misfit_out,
    sens,
    model,
    grad,
    data_grad,
    sums,
    reg_part,
    w_small,
    w_z,
    w_y,
    w_x,
    observed,
    data_weight,
    active,
    links,
    is_active,
    face_small,
    face_z,
    face_y,
    face_x,
    first_z,
    first_y,
    low_z,
    ask,
    asked,
    asked_s,
    slot_row,
    entry_rows,
    slot_of,
    entry_of,
    picked,
    product,
    residual,
    step_pred,
    sent1,
    sent2,
    sent3,
    sent4,
    sent5,
    came1,
    came2,
    came3,
    came4,
    came5,
    spread,
    one_hot,
    stage_y,
    stage_grad_z,
    stage_grad_y,
    halo_z,
    halo_y,
    grad_z,
    grad_y,
    sum_mine,
    sum_a,
    sum_b,
    load_sem,
    send_sem,
    recv_sem,
):
    regions, surveys, layers, rows, tiles, width, slots = dims
    owners = regions * surveys
    cells = layers * rows
    depth_count = float(layers * regions)
    region, survey = lax.axis_index("region"), lax.axis_index("survey")
    me = region * surveys + survey

    def device(flat):
        return (flat // surveys, flat % surveys)

    sent = (None, sent1, sent2, sent3, sent4, sent5)
    came = (None, came1, came2, came3, came4, came5)
    barrier = pltpu.get_barrier_semaphore()

    def greet(i, c):
        pl.semaphore_signal(
            barrier, inc=1, device_id=device((me + i) % owners), device_id_type=MESH
        )
        return c

    lax.fori_loop(1, owners, greet, 0)
    def load(src, dst, number):
        copy = pltpu.make_async_copy(src, dst, load_sem.at[number])
        copy.start()
        return copy

    load_links = load(links_hbm, links, 0)
    load_active = load(active_hbm, active, 1)
    load_model = load(model_hbm, model, 2)
    load_observed = load(observed_hbm, observed, 3)
    load_weight = load(data_weight_hbm, data_weight, 4)
    load_sens = load(sens_hbm, sens, 5)

    entries = tiles * width
    wanted = jnp.concatenate([bricks[t : t + 1, :] for t in range(tiles)], axis=1)
    wanted = jnp.broadcast_to(wanted, (entries, entries))
    upright = lax.broadcasted_iota(jnp.int32, (entries, entries), 0)
    across = lax.broadcasted_iota(jnp.int32, (entries, entries), 1)
    owner = lax.shift_right_logical(wanted, cells.bit_length() - 1)
    local = jnp.bitwise_and(wanted, cells - 1)

    def count(hit, value, axis):
        return jnp.sum(jnp.where(hit, value, 0), axis=axis, keepdims=True)

    def square(line):
        return jnp.broadcast_to(line, (entries, entries))

    owner_col = square(count(upright == across, owner, 1))
    same = owner == owner_col
    rank_col = square(count(same & (across < upright), 1, 1))
    rank_row = square(count(same & (upright < across), 1, 0))
    slot_row[...] = jnp.minimum(2 * owner + rank_row, 2 * owners - 1)[0:1, :]
    mine = owner == upright
    theirs = owner_col == across
    table = jnp.zeros((owners, 128), jnp.int32)
    for rank in range(2):
        number = count(mine & (rank_row == rank), local + 1, 1) - 1
        table = jnp.where(across == rank, jnp.maximum(number, 0), table)
        table = jnp.where(across == 2 + rank, number, table)
        entry_rows[rank : rank + 1, :] = count(theirs & (rank_col == rank), upright, 0)
    ask[...] = table.reshape(owners, 1, 128)
    load_slots = load(slot_row, slot_of, 6)
    load_entries = load(entry_rows, entry_of, 7)
    pl.semaphore_wait(barrier, owners - 1)

    def remote(src, dst, number, to):
        return pltpu.make_async_remote_copy(
            src_ref=src,
            dst_ref=dst,
            send_sem=send_sem.at[number],
            recv_sem=recv_sem.at[number],
            device_id=to,
            device_id_type=MESH,
        )

    def await_bytes(ref, sem):
        pltpu.make_async_copy(ref, ref, sem).wait()

    def send_ids(i, c):
        to = (me + i) % owners
        remote(ask.at[to], asked.at[me], 0, device(to)).start()
        return c

    lax.fori_loop(1, owners, send_ids, 0)
    asked[me] = ask[me]

    def row_of(ref, b):
        return jnp.broadcast_to(ref[pl.ds(b, 1), :], (8, 128))

    z_base = (region * layers).astype(F32)

    load_links.wait()
    load_active.wait()

    def prepare(z, c):
        depth = z_base + z.astype(F32)
        h_here = 1.0 + 2.0 * depth / depth_count
        h_next = 1.0 + (2.0 * depth + 1.0) / depth_count
        for y in range(0, rows, 8):
            at = pl.ds(pl.multiple_of(z * rows + y, 8), 8)
            word = links[at, :]
            alive = active[at, :].astype(F32)

            def faces(k, h):
                return jnp.where(jnp.bitwise_and(word, 2**k) != 0, h, 0.0)

            is_active[at, :] = alive
            face_small[at, :] = alive * h_here
            face_z[at, :] = faces(1, h_next)
            face_y[at, :] = faces(3, h_here)
            face_x[at, :] = faces(5, h_here)
            if y == 0:
                first_y[pl.ds(pl.multiple_of(z * 8, 8), 8), :] = faces(2, h_here)
        return c

    lax.fori_loop(0, layers, prepare, 0)
    for y in range(0, rows, 8):
        word = links[y : y + 8, :]
        first_z[y : y + 8, :] = jnp.where(
            jnp.bitwise_and(word, 1) != 0, 1.0 + (2.0 * z_base - 1.0) / depth_count, 0.0
        )

    load_model.wait()

    def mask_model(b, c):
        model[b] = model[b] * row_of(is_active, b)
        return c

    lax.fori_loop(0, cells, mask_model, 0, unroll=8)

    up_z = ((region + 1) % regions, survey)
    down_z = ((region + regions - 1) % regions, survey)
    up_y = (region, (survey + 1) % surveys)
    down_y = (region, (survey + surveys - 1) % surveys)

    def send_halo(field, into_z, into_y, base):
        for z in range(layers):
            stage_y[0, z] = field[z * rows]
            stage_y[1, z] = field[z * rows + rows - 1]
        last = (layers - 1) * rows
        remote(field.at[pl.ds(0, rows)], into_z.at[1], base, down_z).start()
        remote(field.at[pl.ds(last, rows)], into_z.at[0], base + 1, up_z).start()
        remote(stage_y.at[0], into_y.at[1], base + 2, down_y).start()
        remote(stage_y.at[1], into_y.at[0], base + 3, up_y).start()

    def send_grad_halo(base, side, stage):
        for y in range(rows):
            stage_grad_z[stage, y] = grad[side * (layers - 1) * rows + y].astype(BF16)
        for z in range(layers):
            stage_grad_y[stage, z] = grad[z * rows + side * (rows - 1)].astype(BF16)
        to_z, to_y = (up_z, up_y) if side else (down_z, down_y)
        remote(stage_grad_z.at[stage], grad_z.at[stage], base, to_z).start()
        remote(stage_grad_y.at[stage], grad_y.at[stage], base + 1, to_y).start()

    def await_grad_halo(sems, base, stage):
        await_bytes(grad_z.at[stage], sems.at[base])
        await_bytes(grad_y.at[stage], sems.at[base + 1])

    def await_halo(into_z, into_y, base):
        await_bytes(into_z.at[1], recv_sem.at[base])
        await_bytes(into_z.at[0], recv_sem.at[base + 1])
        await_bytes(into_y.at[1], recv_sem.at[base + 2])
        await_bytes(into_y.at[0], recv_sem.at[base + 3])

    def sent_halo(field, base):
        await_bytes(field.at[pl.ds(0, rows)], send_sem.at[base])
        await_bytes(field.at[pl.ds(0, rows)], send_sem.at[base + 1])
        await_bytes(stage_y.at[0], send_sem.at[base + 2])
        await_bytes(stage_y.at[1], send_sem.at[base + 3])

    send_halo(model, halo_z, halo_y, 10)

    await_bytes(asked.at[pl.ds(0, owners - 1)], recv_sem.at[0])
    load(asked, asked_s, 8).wait()
    load_slots.wait()
    load_entries.wait()

    def exchange(number, first_of, second_of):
        def send(i, c):
            to = (me + i) % owners
            sent[number][2 * to] = first_of(to)
            sent[number][2 * to + 1] = second_of(to)
            two = pl.ds(2 * to, 2)
            remote(
                sent[number].at[two], came[number].at[pl.ds(2 * me, 2)], number, device(to)
            ).start()
            return c

        lax.fori_loop(1, owners, send, 0)
        came[number][2 * me] = first_of(me)
        came[number][2 * me + 1] = second_of(me)

    def fetch(field, number):
        exchange(
            number,
            lambda to: field[asked_s[to, 0, 0]].astype(BF16),
            lambda to: field[asked_s[to, 0, 1]].astype(BF16),
        )

    def give_back(number):
        exchange(
            number,
            lambda to: product[entry_of[0, to]].astype(BF16),
            lambda to: product[entry_of[1, to]].astype(BF16),
        )

    def await_round(number):
        await_bytes(came[number].at[pl.ds(0, 2 * owners - 2)], recv_sem.at[number])

    fetch(model, 1)

    ids = jnp.transpose(asked[:, 0, :].astype(F32))
    numbers = lax.broadcasted_iota(jnp.int32, (cells, owners), 0).astype(F32)
    for rank in range(2):
        named = jnp.broadcast_to(ids[2 + rank : 3 + rank, :], (cells, owners))
        one_hot[:, rank * owners : (rank + 1) * owners] = jnp.where(
            numbers == named, 1.0, 0.0
        ).astype(BF16)

    lane = lax.broadcasted_iota(jnp.int32, (8, 128), 1)
    sample = lax.broadcasted_iota(jnp.int32, (8, 128), 0)
    scale = jnp.zeros((8, 128), F32)
    for s in range(8):
        scale = jnp.where(sample == s, reg_weight[s], scale)

    def regularize():
        def flux(difference, face):
            weight = face * lax.rsqrt(difference * difference + EPS_SQ)
            return weight, weight * difference

        for y in range(rows):
            low_z[y] = flux(model[y] - halo_z[0, y], row_of(first_z, y))[1]

        def one_layer(z, c, last):
            first = model[z * rows]
            _, before = flux(first - halo_y[0, z], row_of(first_y, z * 8))
            for y in range(rows):
                b = z * rows + y
                here = model[b]
                above = halo_z[1, y] if last else model[b + rows]
                beside = model[b + 1] if y < rows - 1 else halo_y[1, z]
                small = row_of(face_small, b) * lax.rsqrt(here * here + EPS_SQ)
                wz, fz = flux(above - here, row_of(face_z, b))
                wy, fy = flux(beside - here, row_of(face_y, b))
                wx, fx = flux(pltpu.roll(here, 127, 1) - here, row_of(face_x, b))
                total = (
                    small * here
                    + (low_z[y] - fz)
                    + (before - fy)
                    + (pltpu.roll(fx, 1, 1) - fx)
                )
                reg_part[b] = scale * total
                w_small[b] = small
                w_z[b] = wz
                w_y[b] = wy
                w_x[b] = wx
                low_z[y] = fz
                before = fy
            return c

        lax.fori_loop(0, layers - 1, functools.partial(one_layer, last=False), 0)
        one_layer(layers - 1, 0, True)

    def curvature(after):
        def one_layer(z, carry, last):
            norm, curv = carry
            for y in range(rows):
                b = z * rows + y
                here = grad[b]
                if last:
                    above = grad_z[after, y].astype(F32)
                else:
                    above = grad[b + rows]
                beside = grad[b + 1] if y < rows - 1 else grad_y[after, z].astype(F32)
                dz, dy, dx = above - here, beside - here, pltpu.roll(here, 127, 1) - here
                square = here * here
                norm = norm + square
                curv = curv + (
                    (w_small[b] * square + w_z[b] * (dz * dz))
                    + (w_y[b] * (dy * dy) + w_x[b] * (dx * dx))
                )
            return norm, curv

        zero = jnp.zeros((8, 128), F32)
        carry = lax.fori_loop(
            0, layers - 1, functools.partial(one_layer, last=False), (zero, zero)
        )
        norm, curv = one_layer(layers - 1, carry, True)
        return (
            jnp.sum(norm, axis=1, keepdims=True),
            jnp.sum(curv * scale, axis=1, keepdims=True),
        )

    def forward(t, number):
        for e in range(width):
            picked[t, :, e * 128 : (e + 1) * 128] = came[number][
                slot_of[0, t * width + e]
            ].astype(F32)
        these = picked[t].astype(BF16)
        block = 256
        made = [
            jnp.transpose(
                lax.dot_general(
                    sens[t, d : d + block, :],
                    these,
                    (((1,), (1,)), ((), ())),
                    preferred_element_type=F32,
                )
            )
            for d in range(0, slots, block)
        ]
        return jnp.concatenate(made, axis=1)

    def backward(t, weighted):
        chunk = 1024
        for c in range(width * 128 // chunk):
            made = lax.dot_general(
                weighted,
                sens[t, :, c * chunk : (c + 1) * chunk],
                (((1,), (0,)), ((), ())),
                preferred_element_type=F32,
            )
            for j in range(chunk // 128):
                entry = t * width + c * (chunk // 128) + j
                product[entry] = made[:, j * 128 : (j + 1) * 128]

    def mask_of(t):
        slot = lax.broadcasted_iota(jnp.int32, (1, slots), 1)
        return jnp.where(slot < counts[t], 1.0, 0.0)

    def weight_of(t):
        weight = data_weight[pl.ds(t, 1), :]
        return mask_of(t) * (weight * weight)

    def scatter(number):
        def widen(d, c):
            spread[pl.ds(pl.multiple_of(d * 8, 8), 8), :] = came[number][d].astype(F32)
            return c

        lax.fori_loop(0, 2 * owners, widen, 0, unroll=8)
        table = one_hot[...]
        for s in range(8):
            first = spread[pl.ds(s, owners, stride=16), :]
            second = spread[pl.ds(8 + s, owners, stride=16), :]
            blocks = jnp.concatenate([first, second], axis=0).astype(BF16)
            sums[pl.ds(s, cells, stride=8), :] = jnp.dot(
                table, blocks, preferred_element_type=F32
            )

    def make_gradient(step):
        def one(b, c):
            total = sums[pl.ds(pl.multiple_of(b * 8, 8), 8), :]
            if step is None:
                data_grad[b] = total
            else:
                total = data_grad[b] - step * total
            grad[b] = row_of(is_active, b) * total + reg_part[b]
            return c

        lax.fori_loop(0, cells, one, 0, unroll=8)

    def sum_start(mine, number):
        sum_mine[number, 0] = mine
        sum_a[number, survey] = mine

        def send(i, c):
            to = (survey + i) % surveys
            remote(
                sum_mine.at[number, 0], sum_a.at[number, survey], 6 + 2 * number, (region, to)
            ).start()
            return c

        lax.fori_loop(1, surveys, send, 0)

    def sum_middle(number):
        await_bytes(sum_a.at[number, pl.ds(0, surveys - 1)], recv_sem.at[6 + 2 * number])
        part = sum_a[number, 0]
        for i in range(1, surveys):
            part = part + sum_a[number, i]
        sum_mine[number, 1] = part
        sum_b[number, region] = part

        def send(i, c):
            to = (region + i) % regions
            remote(
                sum_mine.at[number, 1], sum_b.at[number, region], 7 + 2 * number, (to, survey)
            ).start()
            return c

        lax.fori_loop(1, regions, send, 0)

    def sum_end(number):
        await_bytes(sum_b.at[number, pl.ds(0, regions - 1)], recv_sem.at[7 + 2 * number])
        whole = sum_b[number, 0]
        for i in range(1, regions):
            whole = whole + sum_b[number, i]
        norm = jnp.sum(jnp.where(lane == 0, whole, 0.0), axis=1, keepdims=True)
        curv = jnp.sum(jnp.where(lane == 1, whole, 0.0), axis=1, keepdims=True)
        return norm / curv

    def my_sums(norm, reg_curv, data_curv):
        return jnp.where(lane == 0, norm, jnp.where(lane == 1, reg_curv + data_curv, 0.0))

    await_halo(halo_z, halo_y, 10)
    regularize()
    load_sens.wait()
    load_observed.wait()
    load_weight.wait()

    await_round(1)
    for t in range(tiles):
        gap = forward(t, 1) - observed[t]
        residual[t] = gap
        backward(t, (weight_of(t) * gap).astype(BF16))
    give_back(2)
    await_round(2)
    scatter(2)
    make_gradient(None)
    send_grad_halo(14, 0, 0)
    send_grad_halo(16, 1, 1)
    fetch(grad, 3)
    await_grad_halo(recv_sem, 14, 0)
    await_grad_halo(recv_sem, 16, 1)
    norm, reg_curv = curvature(0)

    await_round(3)
    data_curv = jnp.zeros((8, 1), F32)
    for t in range(tiles):
        made = forward(t, 3)
        step_pred[t] = made
        data_curv = data_curv + jnp.sum(weight_of(t) * made * made, axis=1, keepdims=True)
    sum_start(my_sums(norm, reg_curv, data_curv), 0)
    for t in range(tiles):
        backward(t, (weight_of(t) * step_pred[t]).astype(BF16))
    sum_middle(0)
    give_back(4)
    step = sum_end(0)
    sent_halo(model, 10)
    step_row = jnp.broadcast_to(step, (8, 128))

    def move(b, c):
        model[b] = model[b] - step_row * grad[b]
        return c

    lax.fori_loop(0, cells, move, 0, unroll=8)
    for side in range(2):
        for y in range(rows):
            halo_z[side, y] = halo_z[side, y] - step_row * grad_z[1 - side, y].astype(F32)
        for z in range(layers):
            halo_y[side, z] = halo_y[side, z] - step_row * grad_y[1 - side, z].astype(F32)
    save_model = load(model, model_out, 9)
    regularize()
    for t in range(tiles):
        residual[t] = residual[t] - step * step_pred[t]

    await_round(4)
    scatter(4)
    make_gradient(step_row)
    send_grad_halo(18, 0, 2)
    fetch(grad, 5)
    save_grad = load(grad, grad_out, 10)
    await_grad_halo(recv_sem, 18, 2)
    norm, reg_curv = curvature(2)

    await_round(5)
    data_curv = jnp.zeros((8, 1), F32)
    for t in range(tiles):
        made = forward(t, 5)
        step_pred[t] = made
        data_curv = data_curv + jnp.sum(weight_of(t) * made * made, axis=1, keepdims=True)
    sum_start(my_sums(norm, reg_curv, data_curv), 1)
    sum_middle(1)
    step = sum_end(1)
    step_out[...] = jnp.broadcast_to(step, (8, 128))
    for t in range(tiles):
        weight = mask_of(t) * data_weight[pl.ds(t, 1), :]
        misfit_out[t] = weight * (residual[t] - step * step_pred[t])

    await_bytes(ask.at[pl.ds(0, owners - 1)], send_sem.at[0])
    for number in range(1, 6):
        await_bytes(sent[number].at[pl.ds(0, 2 * owners - 2)], send_sem.at[number])
    for number in range(2):
        await_bytes(sum_a.at[number, pl.ds(0, surveys - 1)], send_sem.at[6 + 2 * number])
        await_bytes(sum_b.at[number, pl.ds(0, regions - 1)], send_sem.at[7 + 2 * number])
    for stage in range(3):
        await_grad_halo(send_sem, 14 + 2 * stage, stage)
    save_model.wait()
    save_grad.wait()


def finish(moved, gradient, step, misfit, final_out, misfit_out, made, sem):
    parts = made.shape[0]
    size = made.shape[1]
    copy_misfit = pltpu.make_async_copy(misfit, misfit_out, sem.at[parts])
    copy_misfit.start()
    copies = []
    for i in range(parts):
        for b in range(size):
            made[i, b] = moved[i * size + b] - step[...] * gradient[i * size + b]
        copies.append(
            pltpu.make_async_copy(made.at[i], final_out.at[pl.ds(i * size, size)], sem.at[i])
        )
        copies[-1].start()
    for copy in copies:
        copy.wait()
    copy_misfit.wait()


def shards(
    regions,
    surveys,
    sensitivity,
    observed,
    data_weight,
    data_counts,
    tile_bricks,
    start_model,
    active_cells,
    face_links,
    reg_weight,
):
    layers, rows, samples, across = start_model.shape
    tiles, width = tile_bricks.shape
    slots = sensitivity.shape[1]
    owners, cells = regions * surveys, layers * rows
    entries = tiles * width

    field = jax.ShapeDtypeStruct((cells, samples, across), F32)
    field_scratch = pltpu.VMEM(field.shape, F32)
    blocks = pltpu.VMEM((2 * owners, samples, across), BF16)
    data_scratch = pltpu.VMEM((tiles, samples, slots), F32)
    plane = pltpu.VMEM((cells, across), F32)
    vmem = pl.BlockSpec(memory_space=pltpu.VMEM)
    smem = pl.BlockSpec(memory_space=pltpu.SMEM)
    anywhere = pl.BlockSpec(memory_space=pl.ANY)
    in_hbm = pl.BlockSpec(memory_space=pltpu.HBM)
    moved, gradient, step, misfit = pl.pallas_call(
        functools.partial(kernel, (regions, surveys, layers, rows, tiles, width, slots)),
        name="inversion",
        out_shape=(
            field,
            field,
            jax.ShapeDtypeStruct((samples, across), F32),
            jax.ShapeDtypeStruct((tiles, samples, slots), F32),
        ),
        in_specs=[smem] * 2 + [vmem] + [in_hbm] * 6,
        out_specs=(anywhere, anywhere, vmem, vmem),
        scratch_shapes=[
            pltpu.VMEM(sensitivity.shape, BF16),
            field_scratch,
            field_scratch,
            field_scratch,
            pltpu.VMEM((cells * samples, across), F32),
            *[field_scratch] * 5,
            pltpu.VMEM(observed.shape, F32),
            pltpu.VMEM(data_weight.shape, F32),
            pltpu.VMEM((cells, across), jnp.int32),
            pltpu.VMEM((cells, across), jnp.int32),
            *[plane] * 5,
            pltpu.VMEM((rows, across), F32),
            pltpu.VMEM((layers * 8, across), F32),
            pltpu.VMEM((rows, 8, 128), F32),
            pltpu.VMEM((owners, 1, 128), jnp.int32),
            pltpu.VMEM((owners, 1, 128), jnp.int32),
            pltpu.SMEM((owners, 1, 128), jnp.int32),
            pltpu.VMEM((1, entries), jnp.int32),
            pltpu.VMEM((2, owners), jnp.int32),
            pltpu.SMEM((1, entries), jnp.int32),
            pltpu.SMEM((2, owners), jnp.int32),
            pltpu.VMEM((tiles, samples, width * 128), F32),
            pltpu.VMEM((entries, samples, across), F32),
            data_scratch,
            data_scratch,
            *[blocks] * 10,
            pltpu.VMEM((owners * 16, 128), F32),
            pltpu.VMEM((cells, 2 * owners), BF16),
            pltpu.VMEM((2, layers, 8, 128), F32),
            pltpu.VMEM((3, rows, 8, 128), BF16),
            pltpu.VMEM((3, layers, 8, 128), BF16),
            pltpu.VMEM((2, rows, 8, 128), F32),
            pltpu.VMEM((2, layers, 8, 128), F32),
            pltpu.VMEM((3, rows, 8, 128), BF16),
            pltpu.VMEM((3, layers, 8, 128), BF16),
            pltpu.VMEM((2, 2, 8, 128), F32),
            pltpu.VMEM((2, surveys, 8, 128), F32),
            pltpu.VMEM((2, regions, 8, 128), F32),
            pltpu.SemaphoreType.DMA((12,)),
            pltpu.SemaphoreType.DMA((20,)),
            pltpu.SemaphoreType.DMA((20,)),
        ],
        compiler_params=pltpu.CompilerParams(
            collective_id=0, has_side_effects=True, vmem_limit_bytes=49 << 20
        ),
    )(
        *(
            pltpu.with_memory_space_constraint(x, pltpu.HBM)
            for x in (
                data_counts,
                reg_weight,
                tile_bricks,
                observed,
                data_weight,
                active_cells.reshape(cells, across),
                face_links.reshape(cells, across),
                start_model.reshape(cells, samples, across),
                sensitivity,
            )
        )
    )
    parts = 8
    final, misfit = pl.pallas_call(
        finish,
        name="finish",
        out_shape=(field, jax.ShapeDtypeStruct(misfit.shape, F32)),
        in_specs=[vmem] * 4,
        out_specs=(in_hbm, in_hbm),
        scratch_shapes=[
            pltpu.VMEM((parts, cells // parts, samples, across), F32),
            pltpu.SemaphoreType.DMA((parts + 1,)),
        ],
        compiler_params=pltpu.CompilerParams(vmem_limit_bytes=8 << 20),
    )(moved, gradient, step, misfit)
    return final.reshape(start_model.shape), misfit


def solution(mesh):
    return jax.shard_map(
        functools.partial(shards, mesh.shape["region"], mesh.shape["survey"]),
        mesh=mesh,
        in_specs=(
            P(("region", "survey"), None, None),
            P(("region", "survey"), None, None),
            P(("region", "survey"), None),
            P(("region", "survey")),
            P(("region", "survey"), None),
            P("region", "survey", None, None),
            P("region", "survey", None),
            P("region", "survey", None),
            P(),
        ),
        out_specs=(P("region", "survey", None, None), P(("region", "survey"), None, None)),
        check_vma=False,
    )
```

```python
import functools

import jax
import jax.numpy as jnp
from jax import lax
from jax.experimental import pallas as pl
from jax.experimental.pallas import tpu as pltpu
from jax.sharding import PartitionSpec as P

MESH = pl.DeviceIdType.MESH
EPS_SQ = 0.09
F32, BF16 = jnp.float32, jnp.bfloat16


def kernel(
    dims,
    counts,
    reg_weight,
    bricks,
    observed_hbm,
    data_weight_hbm,
    active_hbm,
    links_hbm,
    model_hbm,
    sens_hbm,
    model_out,
    grad_out,
    step_out,
    misfit_out,
    sens,
    sens_t,
    model,
    grad,
    sums,
    reg_part,
    observed,
    data_weight,
    active,
    links,
    is_active,
    face_small,
    face_z,
    face_y,
    face_x,
    first_z,
    first_y,
    low_z,
    ask,
    asked,
    asked_rows,
    asked_s,
    slot_row,
    entry_rows,
    slot_of,
    entry_of,
    picked,
    product,
    residual,
    step_pred,
    sent1,
    sent2,
    came1,
    came2,
    spread,
    one_hot,
    stage_y,
    stage_grad_z,
    stage_grad_y,
    halo_z,
    halo_y,
    grad_z,
    grad_y,
    sum_mine,
    sum_a,
    sum_b,
    load_sem,
    send_sem,
    recv_sem,
):
    regions, surveys, layers, rows, tiles, width, slots = dims
    owners = regions * surveys
    cells = layers * rows
    depth_count = float(layers * regions)
    region, survey = lax.axis_index("region"), lax.axis_index("survey")
    me = region * surveys + survey

    def device(flat):
        return (flat // surveys, flat % surveys)

    sent = (sent2, sent1) * 3
    came = (came2, came1) * 3
    barrier = pltpu.get_barrier_semaphore()

    def greet(i, c):
        pl.semaphore_signal(
            barrier, inc=1, device_id=device((me + i) % owners), device_id_type=MESH
        )
        return c

    lax.fori_loop(1, owners, greet, 0)
    def load(src, dst, number):
        copy = pltpu.make_async_copy(src, dst, load_sem.at[number])
        copy.start()
        return copy

    load_links = load(links_hbm, links, 0)
    load_active = load(active_hbm, active, 1)
    load_model = load(model_hbm, model, 2)
    load_observed = load(observed_hbm, observed, 3)
    load_weight = load(data_weight_hbm, data_weight, 4)
    load_sens = [load(sens_hbm.at[t], sens.at[t], 5 + t) for t in range(tiles)]

    entries = tiles * width
    wanted = jnp.concatenate([bricks[t : t + 1, :] for t in range(tiles)], axis=1)
    wanted = jnp.broadcast_to(wanted, (entries, entries))
    upright = lax.broadcasted_iota(jnp.int32, (entries, entries), 0)
    across = lax.broadcasted_iota(jnp.int32, (entries, entries), 1)
    owner = lax.shift_right_logical(wanted, cells.bit_length() - 1)
    local = jnp.bitwise_and(wanted, cells - 1)

    def count(hit, value, axis):
        return jnp.sum(jnp.where(hit, value, 0), axis=axis, keepdims=True)

    def square(line):
        return jnp.broadcast_to(line, (entries, entries))

    owner_col = square(count(upright == across, owner, 1))
    same = owner == owner_col
    rank_col = square(count(same & (across < upright), 1, 1))
    rank_row = square(count(same & (upright < across), 1, 0))
    slot_row[...] = jnp.minimum(2 * owner + rank_row, 2 * owners - 1)[0:1, :]
    mine = owner == upright
    theirs = owner_col == across
    table = jnp.zeros((owners, 128), jnp.int32)
    for rank in range(2):
        number = count(mine & (rank_row == rank), local + 1, 1) - 1
        table = jnp.where(across == rank, jnp.maximum(number, 0), table)
        table = jnp.where(across == 2 + rank, number, table)
        entry_rows[rank : rank + 1, :] = count(theirs & (rank_col == rank), upright, 0)
    ask[...] = table.reshape(owners, 1, 128)
    load_slots = load(slot_row, slot_of, 9)
    load_entries = load(entry_rows, entry_of, 10)
    pl.semaphore_wait(barrier, owners - 1)

    def remote(src, dst, number, to):
        return pltpu.make_async_remote_copy(
            src_ref=src,
            dst_ref=dst,
            send_sem=send_sem.at[number],
            recv_sem=recv_sem.at[number],
            device_id=to,
            device_id_type=MESH,
        )

    def await_bytes(ref, sem):
        pltpu.make_async_copy(ref, ref, sem).wait()

    def send_ids(i, c):
        to = (me + i) % owners
        remote(ask.at[to], asked.at[me], 0, device(to)).start()
        return c

    lax.fori_loop(1, owners, send_ids, 0)
    asked[me] = ask[me]

    def row_of(ref, b):
        return jnp.broadcast_to(ref[pl.ds(b, 1), :], (8, 128))

    z_base = (region * layers).astype(F32)

    load_links.wait()
    load_active.wait()

    def prepare(z, c):
        depth = z_base + z.astype(F32)
        h_here = 1.0 + 2.0 * depth / depth_count
        h_next = 1.0 + (2.0 * depth + 1.0) / depth_count
        for y in range(0, rows, 8):
            at = pl.ds(pl.multiple_of(z * rows + y, 8), 8)
            word = links[at, :]
            alive = active[at, :].astype(F32)

            def faces(k, h):
                return jnp.where(jnp.bitwise_and(word, 2**k) != 0, h, 0.0)

            is_active[at, :] = alive
            face_small[at, :] = alive * h_here
            face_z[at, :] = faces(1, h_next)
            face_y[at, :] = faces(3, h_here)
            face_x[at, :] = faces(5, h_here)
            if y == 0:
                first_y[pl.ds(pl.multiple_of(z * 8, 8), 8), :] = faces(2, h_here)
        return c

    lax.fori_loop(0, layers, prepare, 0)
    for y in range(0, rows, 8):
        word = links[y : y + 8, :]
        first_z[y : y + 8, :] = jnp.where(
            jnp.bitwise_and(word, 1) != 0, 1.0 + (2.0 * z_base - 1.0) / depth_count, 0.0
        )

    load_model.wait()

    def mask_model(b, c):
        model[b] = model[b] * row_of(is_active, b)
        return c

    lax.fori_loop(0, cells, mask_model, 0, unroll=8)

    up_z = ((region + 1) % regions, survey)
    down_z = ((region + regions - 1) % regions, survey)
    up_y = (region, (survey + 1) % surveys)
    down_y = (region, (survey + surveys - 1) % surveys)

    def send_halo(field, into_z, into_y, base):
        for z in range(layers):
            stage_y[0, z] = field[z * rows]
            stage_y[1, z] = field[z * rows + rows - 1]
        last = (layers - 1) * rows
        remote(field.at[pl.ds(0, rows)], into_z.at[1], base, down_z).start()
        remote(field.at[pl.ds(last, rows)], into_z.at[0], base + 1, up_z).start()
        remote(stage_y.at[0], into_y.at[1], base + 2, down_y).start()
        remote(stage_y.at[1], into_y.at[0], base + 3, up_y).start()

    def send_grad_halo(base, side, stage):
        for y in range(rows):
            stage_grad_z[stage, y] = grad[side * (layers - 1) * rows + y].astype(BF16)
        for z in range(layers):
            stage_grad_y[stage, z] = grad[z * rows + side * (rows - 1)].astype(BF16)
        to_z, to_y = (up_z, up_y) if side else (down_z, down_y)
        remote(stage_grad_z.at[stage], grad_z.at[stage], base, to_z).start()
        remote(stage_grad_y.at[stage], grad_y.at[stage], base + 1, to_y).start()

    def await_grad_halo(sems, base, stage):
        await_bytes(grad_z.at[stage], sems.at[base])
        await_bytes(grad_y.at[stage], sems.at[base + 1])

    def await_halo(into_z, into_y, base):
        await_bytes(into_z.at[1], recv_sem.at[base])
        await_bytes(into_z.at[0], recv_sem.at[base + 1])
        await_bytes(into_y.at[1], recv_sem.at[base + 2])
        await_bytes(into_y.at[0], recv_sem.at[base + 3])

    def sent_halo(field, base):
        await_bytes(field.at[pl.ds(0, rows)], send_sem.at[base])
        await_bytes(field.at[pl.ds(0, rows)], send_sem.at[base + 1])
        await_bytes(stage_y.at[0], send_sem.at[base + 2])
        await_bytes(stage_y.at[1], send_sem.at[base + 3])

    send_halo(model, halo_z, halo_y, 10)

    def turn(t):
        load_sens[t].wait()

        def one(c, carry):
            at = pl.ds(pl.multiple_of(c * 512, 512), 512)
            sens_t[t, at, :] = jnp.transpose(sens[t, :, at])
            return carry

        lax.fori_loop(0, width * 128 // 512, one, 0)

    turn(0)
    turn(1)

    await_bytes(asked.at[pl.ds(0, owners - 1)], recv_sem.at[0])
    ids = jnp.transpose(asked[:, 0, :])
    asked_rows[...] = ids[0:2, :]
    load(asked_rows, asked_s, 11).wait()
    load_slots.wait()
    load_entries.wait()

    def exchange(number, first_of, second_of):
        def send(i, c):
            to = (me + i) % owners
            sent[number][2 * to] = first_of(to)
            sent[number][2 * to + 1] = second_of(to)
            two = pl.ds(2 * to, 2)
            remote(
                sent[number].at[two], came[number].at[pl.ds(2 * me, 2)], number, device(to)
            ).start()
            return c

        if number > 2:
            await_bytes(sent[number].at[pl.ds(0, 2 * owners - 2)], send_sem.at[number - 2])
        lax.fori_loop(1, owners, send, 0)
        came[number][2 * me] = first_of(me)
        came[number][2 * me + 1] = second_of(me)

    def fetch(field, number):
        exchange(
            number,
            lambda to: field[asked_s[0, to]].astype(BF16),
            lambda to: field[asked_s[1, to]].astype(BF16),
        )

    def give_back(number):
        exchange(
            number,
            lambda to: product[entry_of[0, to]].astype(BF16),
            lambda to: product[entry_of[1, to]].astype(BF16),
        )

    def await_round(number):
        await_bytes(came[number].at[pl.ds(0, 2 * owners - 2)], recv_sem.at[number])

    fetch(model, 1)

    numbers = lax.broadcasted_iota(jnp.int32, (cells, owners), 0)
    for rank in range(2):
        named = jnp.broadcast_to(ids[2 + rank : 3 + rank, :], (cells, owners))
        one_hot[:, rank * owners : (rank + 1) * owners] = jnp.where(
            numbers == named, 1.0, 0.0
        ).astype(BF16)

    lane = lax.broadcasted_iota(jnp.int32, (8, 128), 1)
    sample = lax.broadcasted_iota(jnp.int32, (8, 128), 0)
    scale = jnp.zeros((8, 128), F32)
    for s in range(8):
        scale = jnp.where(sample == s, reg_weight[s], scale)

    def conduct(difference, face):
        return face * lax.rsqrt(difference * difference + EPS_SQ)

    def regularize(data_part):
        def flux(difference, face):
            return conduct(difference, face) * difference

        for y in range(rows):
            low_z[y] = flux(model[y] - halo_z[0, y], row_of(first_z, y))

        def one_layer(z, c, last):
            first = model[z * rows]
            before = flux(first - halo_y[0, z], row_of(first_y, z * 8))
            for y in range(rows):
                b = z * rows + y
                here = model[b]
                above = halo_z[1, y] if last else model[b + rows]
                beside = model[b + 1] if y < rows - 1 else halo_y[1, z]
                small = conduct(here, row_of(face_small, b))
                fz = flux(above - here, row_of(face_z, b))
                fy = flux(beside - here, row_of(face_y, b))
                fx = flux(pltpu.roll(here, 127, 1) - here, row_of(face_x, b))
                total = (
                    small * here
                    + (low_z[y] - fz)
                    + (before - fy)
                    + (pltpu.roll(fx, 1, 1) - fx)
                )
                total = scale * total
                if data_part:
                    total = total + (grad[b] - reg_part[b])
                reg_part[b] = total
                low_z[y] = fz
                before = fy
            return c

        lax.fori_loop(0, layers - 1, functools.partial(one_layer, last=False), 0)
        one_layer(layers - 1, 0, True)

    def curvature(after, base):
        def one_layer(z, carry, last):
            norm, curv = carry
            for y in range(rows):
                b = z * rows + y
                here, cell = grad[b], model[b]
                square = here * here
                norm = norm + square
                dx = pltpu.roll(here, 127, 1) - here
                part = conduct(cell, row_of(face_small, b)) * square
                part = part + conduct(
                    pltpu.roll(cell, 127, 1) - cell, row_of(face_x, b)
                ) * (dx * dx)
                if not last:
                    dz = grad[b + rows] - here
                    part = part + conduct(model[b + rows] - cell, row_of(face_z, b)) * (dz * dz)
                if y < rows - 1:
                    dy = grad[b + 1] - here
                    part = part + conduct(model[b + 1] - cell, row_of(face_y, b)) * (dy * dy)
                curv = curv + part
            return norm, curv

        zero = jnp.zeros((8, 128), F32)
        carry = lax.fori_loop(
            0, layers - 1, functools.partial(one_layer, last=False), (zero, zero)
        )
        norm, curv = one_layer(layers - 1, carry, True)
        await_grad_halo(recv_sem, base, after)
        for y in range(rows):
            b = (layers - 1) * rows + y
            dz = grad_z[after, y].astype(F32) - grad[b]
            curv = curv + conduct(halo_z[1, y] - model[b], row_of(face_z, b)) * (dz * dz)
        for z in range(layers):
            b = z * rows + rows - 1
            dy = grad_y[after, z].astype(F32) - grad[b]
            curv = curv + conduct(halo_y[1, z] - model[b], row_of(face_y, b)) * (dy * dy)
        return (
            jnp.sum(norm, axis=1, keepdims=True),
            jnp.sum(curv * scale, axis=1, keepdims=True),
        )

    def forward(t, number):
        for e in range(width):
            picked[t, :, e * 128 : (e + 1) * 128] = came[number][
                slot_of[0, t * width + e]
            ].astype(F32)
        return jnp.dot(picked[t].astype(BF16), sens_t[t], preferred_element_type=F32)

    def backward(t, weighted):
        chunk = 1024
        for c in range(width * 128 // chunk):
            made = lax.dot_general(
                weighted,
                sens[t, :, c * chunk : (c + 1) * chunk],
                (((1,), (0,)), ((), ())),
                preferred_element_type=F32,
            )
            for j in range(chunk // 128):
                entry = t * width + c * (chunk // 128) + j
                product[entry] = made[:, j * 128 : (j + 1) * 128]

    def mask_of(t):
        slot = lax.broadcasted_iota(jnp.int32, (1, slots), 1)
        return jnp.where(slot < counts[t], 1.0, 0.0)

    def weight_of(t):
        weight = data_weight[pl.ds(t, 1), :]
        return mask_of(t) * (weight * weight)

    def scatter(number):
        def widen(d, c):
            spread[pl.ds(pl.multiple_of(d * 8, 8), 8), :] = came[number][d].astype(F32)
            return c

        lax.fori_loop(0, 2 * owners, widen, 0, unroll=8)
        table = one_hot[...]
        for s in range(8):
            first = spread[pl.ds(s, owners, stride=16), :]
            second = spread[pl.ds(8 + s, owners, stride=16), :]
            blocks = jnp.concatenate([first, second], axis=0).astype(BF16)
            sums[pl.ds(s, cells, stride=8), :] = jnp.dot(
                table, blocks, preferred_element_type=F32
            )

    def make_gradient(step):
        def one(b, c):
            total = row_of(is_active, b) * sums[pl.ds(pl.multiple_of(b * 8, 8), 8), :]
            grad[b] = reg_part[b] + total if step is None else reg_part[b] - step * total
            return c

        lax.fori_loop(0, cells, one, 0, unroll=8)

    def sum_start(mine, number):
        sum_mine[number, 0] = mine
        sum_a[number, survey] = mine

        def send(i, c):
            to = (survey + i) % surveys
            remote(
                sum_mine.at[number, 0], sum_a.at[number, survey], 6 + 2 * number, (region, to)
            ).start()
            return c

        lax.fori_loop(1, surveys, send, 0)

    def sum_middle(number):
        await_bytes(sum_a.at[number, pl.ds(0, surveys - 1)], recv_sem.at[6 + 2 * number])
        part = sum_a[number, 0]
        for i in range(1, surveys):
            part = part + sum_a[number, i]
        sum_mine[number, 1] = part
        sum_b[number, region] = part

        def send(i, c):
            to = (region + i) % regions
            remote(
                sum_mine.at[number, 1], sum_b.at[number, region], 7 + 2 * number, (to, survey)
            ).start()
            return c

        lax.fori_loop(1, regions, send, 0)

    def sum_end(number):
        await_bytes(sum_b.at[number, pl.ds(0, regions - 1)], recv_sem.at[7 + 2 * number])
        whole = sum_b[number, 0]
        for i in range(1, regions):
            whole = whole + sum_b[number, i]
        norm = jnp.sum(jnp.where(lane == 0, whole, 0.0), axis=1, keepdims=True)
        curv = jnp.sum(jnp.where(lane == 1, whole, 0.0), axis=1, keepdims=True)
        return norm / curv

    def my_sums(norm, reg_curv, data_curv):
        return jnp.where(lane == 0, norm, jnp.where(lane == 1, reg_curv + data_curv, 0.0))

    await_halo(halo_z, halo_y, 10)
    regularize(False)
    turn(2)
    turn(3)
    load_observed.wait()
    load_weight.wait()

    await_round(1)
    for t in range(tiles):
        gap = forward(t, 1) - observed[t]
        residual[t] = gap
        backward(t, (weight_of(t) * gap).astype(BF16))
    give_back(2)
    await_round(2)
    scatter(2)
    make_gradient(None)
    send_grad_halo(14, 0, 0)
    fetch(grad, 3)
    norm, reg_curv = curvature(0, 14)

    await_round(3)
    send_grad_halo(16, 1, 1)
    data_curv = jnp.zeros((8, 1), F32)
    for t in range(tiles):
        made = forward(t, 3)
        step_pred[t] = made
        data_curv = data_curv + jnp.sum(weight_of(t) * made * made, axis=1, keepdims=True)
    sum_start(my_sums(norm, reg_curv, data_curv), 0)
    for t in range(tiles):
        backward(t, (weight_of(t) * step_pred[t]).astype(BF16))
    sum_middle(0)
    give_back(4)
    step = sum_end(0)
    sent_halo(model, 10)
    step_row = jnp.broadcast_to(step, (8, 128))

    def move(b, c):
        model[b] = model[b] - step_row * grad[b]
        return c

    lax.fori_loop(0, cells, move, 0, unroll=8)
    await_grad_halo(recv_sem, 16, 1)
    for side in range(2):
        for y in range(rows):
            halo_z[side, y] = halo_z[side, y] - step_row * grad_z[1 - side, y].astype(F32)
        for z in range(layers):
            halo_y[side, z] = halo_y[side, z] - step_row * grad_y[1 - side, z].astype(F32)
    save_model = load(model, model_out, 12)
    regularize(True)
    for t in range(tiles):
        residual[t] = residual[t] - step * step_pred[t]

    await_round(4)
    scatter(4)
    make_gradient(step_row)
    send_grad_halo(18, 0, 2)
    fetch(grad, 5)
    save_grad = load(grad, grad_out, 13)
    norm, reg_curv = curvature(2, 18)

    await_round(5)
    data_curv = jnp.zeros((8, 1), F32)
    for t in range(tiles):
        made = forward(t, 5)
        step_pred[t] = made
        data_curv = data_curv + jnp.sum(weight_of(t) * made * made, axis=1, keepdims=True)
    sum_start(my_sums(norm, reg_curv, data_curv), 1)
    sum_middle(1)
    step = sum_end(1)
    step_out[...] = jnp.broadcast_to(step, (8, 128))
    for t in range(tiles):
        weight = mask_of(t) * data_weight[pl.ds(t, 1), :]
        misfit_out[t] = weight * (residual[t] - step * step_pred[t])

    await_bytes(ask.at[pl.ds(0, owners - 1)], send_sem.at[0])
    for number in range(4, 6):
        await_bytes(sent[number].at[pl.ds(0, 2 * owners - 2)], send_sem.at[number])
    for number in range(2):
        await_bytes(sum_a.at[number, pl.ds(0, surveys - 1)], send_sem.at[6 + 2 * number])
        await_bytes(sum_b.at[number, pl.ds(0, regions - 1)], send_sem.at[7 + 2 * number])
    for stage in range(3):
        await_grad_halo(send_sem, 14 + 2 * stage, stage)
    save_model.wait()
    save_grad.wait()


def finish(moved, gradient, step, misfit, final_out, misfit_out, made, sem):
    parts = made.shape[0]
    size = made.shape[1]
    copy_misfit = pltpu.make_async_copy(misfit, misfit_out, sem.at[parts])
    copy_misfit.start()
    copies = []
    for i in range(parts):
        for b in range(size):
            made[i, b] = moved[i * size + b] - step[...] * gradient[i * size + b]
        copies.append(
            pltpu.make_async_copy(made.at[i], final_out.at[pl.ds(i * size, size)], sem.at[i])
        )
        copies[-1].start()
    for copy in copies:
        copy.wait()
    copy_misfit.wait()


def shards(
    regions,
    surveys,
    sensitivity,
    observed,
    data_weight,
    data_counts,
    tile_bricks,
    start_model,
    active_cells,
    face_links,
    reg_weight,
):
    layers, rows, samples, across = start_model.shape
    tiles, width = tile_bricks.shape
    slots = sensitivity.shape[1]
    owners, cells = regions * surveys, layers * rows
    entries = tiles * width

    field = jax.ShapeDtypeStruct((cells, samples, across), F32)
    field_scratch = pltpu.VMEM(field.shape, F32)
    blocks = pltpu.VMEM((2 * owners, samples, across), BF16)
    data_scratch = pltpu.VMEM((tiles, samples, slots), F32)
    plane = pltpu.VMEM((cells, across), F32)
    vmem = pl.BlockSpec(memory_space=pltpu.VMEM)
    smem = pl.BlockSpec(memory_space=pltpu.SMEM)
    anywhere = pl.BlockSpec(memory_space=pl.ANY)
    in_hbm = pl.BlockSpec(memory_space=pltpu.HBM)
    moved, gradient, step, misfit = pl.pallas_call(
        functools.partial(kernel, (regions, surveys, layers, rows, tiles, width, slots)),
        name="inversion",
        out_shape=(
            field,
            field,
            jax.ShapeDtypeStruct((samples, across), F32),
            jax.ShapeDtypeStruct((tiles, samples, slots), F32),
        ),
        in_specs=[smem] * 2 + [vmem] + [in_hbm] * 6,
        out_specs=(anywhere, anywhere, vmem, vmem),
        scratch_shapes=[
            pltpu.VMEM(sensitivity.shape, BF16),
            pltpu.VMEM((tiles, width * across, slots), BF16),
            field_scratch,
            field_scratch,
            pltpu.VMEM((cells * samples, across), F32),
            field_scratch,
            pltpu.VMEM(observed.shape, F32),
            pltpu.VMEM(data_weight.shape, F32),
            pltpu.VMEM((cells, across), jnp.int32),
            pltpu.VMEM((cells, across), jnp.int32),
            *[plane] * 5,
            pltpu.VMEM((rows, across), F32),
            pltpu.VMEM((layers * 8, across), F32),
            pltpu.VMEM((rows, 8, 128), F32),
            pltpu.VMEM((owners, 1, 128), jnp.int32),
            pltpu.VMEM((owners, 1, 128), jnp.int32),
            pltpu.VMEM((2, owners), jnp.int32),
            pltpu.SMEM((2, owners), jnp.int32),
            pltpu.VMEM((1, entries), jnp.int32),
            pltpu.VMEM((2, owners), jnp.int32),
            pltpu.SMEM((1, entries), jnp.int32),
            pltpu.SMEM((2, owners), jnp.int32),
            pltpu.VMEM((tiles, samples, width * 128), F32),
            pltpu.VMEM((entries, samples, across), F32),
            data_scratch,
            data_scratch,
            *[blocks] * 4,
            pltpu.VMEM((owners * 16, 128), F32),
            pltpu.VMEM((cells, 2 * owners), BF16),
            pltpu.VMEM((2, layers, 8, 128), F32),
            pltpu.VMEM((3, rows, 8, 128), BF16),
            pltpu.VMEM((3, layers, 8, 128), BF16),
            pltpu.VMEM((2, rows, 8, 128), F32),
            pltpu.VMEM((2, layers, 8, 128), F32),
            pltpu.VMEM((3, rows, 8, 128), BF16),
            pltpu.VMEM((3, layers, 8, 128), BF16),
            pltpu.VMEM((2, 2, 8, 128), F32),
            pltpu.VMEM((2, surveys, 8, 128), F32),
            pltpu.VMEM((2, regions, 8, 128), F32),
            pltpu.SemaphoreType.DMA((14,)),
            pltpu.SemaphoreType.DMA((20,)),
            pltpu.SemaphoreType.DMA((20,)),
        ],
        compiler_params=pltpu.CompilerParams(
            collective_id=0, has_side_effects=True, vmem_limit_bytes=97 << 19
        ),
    )(
        *(
            pltpu.with_memory_space_constraint(x, pltpu.HBM)
            for x in (
                data_counts,
                reg_weight,
                tile_bricks,
                observed,
                data_weight,
                active_cells.reshape(cells, across),
                face_links.reshape(cells, across),
                start_model.reshape(cells, samples, across),
                sensitivity,
            )
        )
    )
    parts = 8
    final, misfit = pl.pallas_call(
        finish,
        name="finish",
        out_shape=(field, jax.ShapeDtypeStruct(misfit.shape, F32)),
        in_specs=[vmem] * 4,
        out_specs=(in_hbm, in_hbm),
        scratch_shapes=[
            pltpu.VMEM((parts, cells // parts, samples, across), F32),
            pltpu.SemaphoreType.DMA((parts + 1,)),
        ],
        compiler_params=pltpu.CompilerParams(vmem_limit_bytes=8 << 20),
    )(moved, gradient, step, misfit)
    return final.reshape(start_model.shape), misfit


def solution(mesh):
    return jax.shard_map(
        functools.partial(shards, mesh.shape["region"], mesh.shape["survey"]),
        mesh=mesh,
        in_specs=(
            P(("region", "survey"), None, None),
            P(("region", "survey"), None, None),
            P(("region", "survey"), None),
            P(("region", "survey")),
            P(("region", "survey"), None),
            P("region", "survey", None, None),
            P("region", "survey", None),
            P("region", "survey", None),
            P(),
        ),
        out_specs=(P("region", "survey", None, None), P(("region", "survey"), None, None)),
        check_vma=False,
    )
```

```python
import functools

import jax
import jax.numpy as jnp
from jax import lax
from jax.experimental import pallas as pl
from jax.experimental.pallas import tpu as pltpu
from jax.sharding import PartitionSpec as P

MESH = pl.DeviceIdType.MESH
EPS_SQ = 0.09
F32, BF16 = jnp.float32, jnp.bfloat16


def kernel(
    dims,
    counts,
    reg_weight,
    bricks,
    observed_hbm,
    data_weight_hbm,
    active_hbm,
    links_hbm,
    model_hbm,
    sens_hbm,
    model_out,
    grad_out,
    step_out,
    misfit_out,
    sens,
    sens_t,
    model,
    grad,
    sums,
    reg_part,
    observed,
    data_weight,
    active,
    links,
    is_active,
    face_small,
    face_z,
    face_y,
    face_x,
    first_z,
    first_y,
    low_z,
    ask,
    asked,
    asked_rows,
    asked_s,
    slot_row,
    entry_rows,
    slot_of,
    entry_of,
    picked,
    product,
    residual,
    step_pred,
    sent1,
    sent2,
    came1,
    came2,
    spread,
    one_hot,
    stage_y,
    stage_grad_z,
    stage_grad_y,
    halo_z,
    halo_y,
    grad_z,
    grad_y,
    sum_mine,
    sum_a,
    sum_b,
    load_sem,
    send_sem,
    recv_sem,
):
    regions, surveys, layers, rows, tiles, width, slots = dims
    owners = regions * surveys
    cells = layers * rows
    depth_count = float(layers * regions)
    region, survey = lax.axis_index("region"), lax.axis_index("survey")
    me = region * surveys + survey

    def device(flat):
        return (flat // surveys, flat % surveys)

    sent = (sent2, sent1) * 3
    came = (came2, came1) * 3
    barrier = pltpu.get_barrier_semaphore()

    def greet(i, c):
        pl.semaphore_signal(
            barrier, inc=1, device_id=device((me + i) % owners), device_id_type=MESH
        )
        return c

    lax.fori_loop(1, owners, greet, 0)
    def load(src, dst, number):
        copy = pltpu.make_async_copy(src, dst, load_sem.at[number])
        copy.start()
        return copy

    load_links = load(links_hbm, links, 0)
    load_active = load(active_hbm, active, 1)
    load_model = load(model_hbm, model, 2)
    load_observed = load(observed_hbm, observed, 3)
    load_weight = load(data_weight_hbm, data_weight, 4)
    load_sens = [load(sens_hbm.at[t], sens.at[t], 5 + t) for t in range(tiles)]

    entries = tiles * width
    wanted = jnp.concatenate([bricks[t : t + 1, :] for t in range(tiles)], axis=1)
    wanted = jnp.broadcast_to(wanted, (entries, entries))
    upright = lax.broadcasted_iota(jnp.int32, (entries, entries), 0)
    across = lax.broadcasted_iota(jnp.int32, (entries, entries), 1)
    owner = lax.shift_right_logical(wanted, cells.bit_length() - 1)
    local = jnp.bitwise_and(wanted, cells - 1)

    def count(hit, value, axis):
        return jnp.sum(jnp.where(hit, value, 0), axis=axis, keepdims=True)

    def square(line):
        return jnp.broadcast_to(line, (entries, entries))

    owner_col = square(count(upright == across, owner, 1))
    same = owner == owner_col
    rank_col = square(count(same & (across < upright), 1, 1))
    rank_row = square(count(same & (upright < across), 1, 0))
    slot_row[...] = jnp.minimum(2 * owner + rank_row, 2 * owners - 1)[0:1, :]
    mine = owner == upright
    theirs = owner_col == across
    table = jnp.zeros((owners, 128), jnp.int32)
    for rank in range(2):
        number = count(mine & (rank_row == rank), local + 1, 1) - 1
        table = jnp.where(across == rank, jnp.maximum(number, 0), table)
        table = jnp.where(across == 2 + rank, number, table)
        entry_rows[rank : rank + 1, :] = count(theirs & (rank_col == rank), upright, 0)
    ask[...] = table.reshape(owners, 1, 128)
    load_slots = load(slot_row, slot_of, 9)
    load_entries = load(entry_rows, entry_of, 10)
    pl.semaphore_wait(barrier, owners - 1)

    def remote(src, dst, number, to):
        return pltpu.make_async_remote_copy(
            src_ref=src,
            dst_ref=dst,
            send_sem=send_sem.at[number],
            recv_sem=recv_sem.at[number],
            device_id=to,
            device_id_type=MESH,
        )

    def await_bytes(ref, sem):
        pltpu.make_async_copy(ref, ref, sem).wait()

    def send_ids(i, c):
        to = (me + i) % owners
        remote(ask.at[to], asked.at[me], 0, device(to)).start()
        return c

    lax.fori_loop(1, owners, send_ids, 0)
    asked[me] = ask[me]

    def row_of(ref, b):
        return jnp.broadcast_to(ref[pl.ds(b, 1), :], (8, 128))

    z_base = (region * layers).astype(F32)

    load_links.wait()
    load_active.wait()

    def prepare(z, c):
        depth = z_base + z.astype(F32)
        h_here = 1.0 + 2.0 * depth / depth_count
        h_next = 1.0 + (2.0 * depth + 1.0) / depth_count
        for y in range(0, rows, 8):
            at = pl.ds(pl.multiple_of(z * rows + y, 8), 8)
            word = links[at, :]
            alive = active[at, :].astype(F32)

            def faces(k, h):
                return jnp.where(jnp.bitwise_and(word, 2**k) != 0, h, 0.0)

            is_active[at, :] = alive
            face_small[at, :] = alive * h_here
            face_z[at, :] = faces(1, h_next)
            face_y[at, :] = faces(3, h_here)
            face_x[at, :] = faces(5, h_here)
            if y == 0:
                first_y[pl.ds(pl.multiple_of(z * 8, 8), 8), :] = faces(2, h_here)
        return c

    lax.fori_loop(0, layers, prepare, 0)
    for y in range(0, rows, 8):
        word = links[y : y + 8, :]
        first_z[y : y + 8, :] = jnp.where(
            jnp.bitwise_and(word, 1) != 0, 1.0 + (2.0 * z_base - 1.0) / depth_count, 0.0
        )

    load_model.wait()

    def mask_model(b, c):
        model[b] = model[b] * row_of(is_active, b)
        return c

    lax.fori_loop(0, cells, mask_model, 0, unroll=8)

    up_z = ((region + 1) % regions, survey)
    down_z = ((region + regions - 1) % regions, survey)
    up_y = (region, (survey + 1) % surveys)
    down_y = (region, (survey + surveys - 1) % surveys)

    def send_halo(field, into_z, into_y, base):
        for z in range(layers):
            stage_y[0, z] = field[z * rows]
            stage_y[1, z] = field[z * rows + rows - 1]
        last = (layers - 1) * rows
        remote(field.at[pl.ds(0, rows)], into_z.at[1], base, down_z).start()
        remote(field.at[pl.ds(last, rows)], into_z.at[0], base + 1, up_z).start()
        remote(stage_y.at[0], into_y.at[1], base + 2, down_y).start()
        remote(stage_y.at[1], into_y.at[0], base + 3, up_y).start()

    def send_grad_halo(base, side, stage):
        for y in range(rows):
            stage_grad_z[stage, y] = grad[side * (layers - 1) * rows + y].astype(BF16)
        for z in range(layers):
            stage_grad_y[stage, z] = grad[z * rows + side * (rows - 1)].astype(BF16)
        to_z, to_y = (up_z, up_y) if side else (down_z, down_y)
        remote(stage_grad_z.at[stage], grad_z.at[stage], base, to_z).start()
        remote(stage_grad_y.at[stage], grad_y.at[stage], base + 1, to_y).start()

    def await_grad_halo(sems, base, stage):
        await_bytes(grad_z.at[stage], sems.at[base])
        await_bytes(grad_y.at[stage], sems.at[base + 1])

    def await_halo(into_z, into_y, base):
        await_bytes(into_z.at[1], recv_sem.at[base])
        await_bytes(into_z.at[0], recv_sem.at[base + 1])
        await_bytes(into_y.at[1], recv_sem.at[base + 2])
        await_bytes(into_y.at[0], recv_sem.at[base + 3])

    def sent_halo(field, base):
        await_bytes(field.at[pl.ds(0, rows)], send_sem.at[base])
        await_bytes(field.at[pl.ds(0, rows)], send_sem.at[base + 1])
        await_bytes(stage_y.at[0], send_sem.at[base + 2])
        await_bytes(stage_y.at[1], send_sem.at[base + 3])

    send_halo(model, halo_z, halo_y, 10)

    def turn(t):
        load_sens[t].wait()

        def one(c, carry):
            at = pl.ds(pl.multiple_of(c * 512, 512), 512)
            sens_t[t, at, :] = jnp.transpose(sens[t, :, at])
            return carry

        lax.fori_loop(0, width * 128 // 512, one, 0)

    turn(0)
    turn(1)

    await_bytes(asked.at[pl.ds(0, owners - 1)], recv_sem.at[0])
    ids = jnp.transpose(asked[:, 0, :])
    asked_rows[...] = ids[0:2, :]
    load(asked_rows, asked_s, 11).wait()
    load_slots.wait()
    load_entries.wait()

    def exchange(number, first_of, second_of, between=None):
        def send(i, c):
            to = (me + i) % owners
            sent[number][2 * to] = first_of(to)
            sent[number][2 * to + 1] = second_of(to)
            two = pl.ds(2 * to, 2)
            remote(
                sent[number].at[two], came[number].at[pl.ds(2 * me, 2)], number, device(to)
            ).start()
            return c

        if number > 2:
            await_bytes(sent[number].at[pl.ds(0, 2 * owners - 2)], send_sem.at[number - 2])
        if between is None:
            lax.fori_loop(1, owners, send, 0)
        else:
            early = 3 * owners // 8
            lax.fori_loop(1, early, send, 0)
            between()
            lax.fori_loop(early, owners, send, 0)
        came[number][2 * me] = first_of(me)
        came[number][2 * me + 1] = second_of(me)

    def fetch(field, number):
        exchange(
            number,
            lambda to: field[asked_s[0, to]].astype(BF16),
            lambda to: field[asked_s[1, to]].astype(BF16),
        )

    def give_back(number, between=None):
        exchange(
            number,
            lambda to: product[entry_of[0, to]].astype(BF16),
            lambda to: product[entry_of[1, to]].astype(BF16),
            between,
        )

    def await_round(number):
        await_bytes(came[number].at[pl.ds(0, 2 * owners - 2)], recv_sem.at[number])

    fetch(model, 1)

    numbers = lax.broadcasted_iota(jnp.int32, (cells, owners), 0)
    for rank in range(2):
        named = jnp.broadcast_to(ids[2 + rank : 3 + rank, :], (cells, owners))
        one_hot[:, rank * owners : (rank + 1) * owners] = jnp.where(
            numbers == named, 1.0, 0.0
        ).astype(BF16)

    lane = lax.broadcasted_iota(jnp.int32, (8, 128), 1)
    sample = lax.broadcasted_iota(jnp.int32, (8, 128), 0)
    scale = jnp.zeros((8, 128), F32)
    for s in range(8):
        scale = jnp.where(sample == s, reg_weight[s], scale)

    def conduct(difference, face):
        return face * lax.rsqrt(difference * difference + EPS_SQ)

    def regularize(data_part):
        def flux(difference, face):
            return conduct(difference, face) * difference

        for y in range(rows):
            low_z[y] = flux(model[y] - halo_z[0, y], row_of(first_z, y))

        def one_layer(z, c, last):
            first = model[z * rows]
            before = flux(first - halo_y[0, z], row_of(first_y, z * 8))
            for y in range(rows):
                b = z * rows + y
                here = model[b]
                above = halo_z[1, y] if last else model[b + rows]
                beside = model[b + 1] if y < rows - 1 else halo_y[1, z]
                small = conduct(here, row_of(face_small, b))
                fz = flux(above - here, row_of(face_z, b))
                fy = flux(beside - here, row_of(face_y, b))
                fx = flux(pltpu.roll(here, 127, 1) - here, row_of(face_x, b))
                total = (
                    small * here
                    + (low_z[y] - fz)
                    + (before - fy)
                    + (pltpu.roll(fx, 1, 1) - fx)
                )
                total = scale * total
                if data_part:
                    total = total + (grad[b] - reg_part[b])
                reg_part[b] = total
                low_z[y] = fz
                before = fy
            return c

        lax.fori_loop(0, layers - 1, functools.partial(one_layer, last=False), 0)
        one_layer(layers - 1, 0, True)

    def curvature():
        def one_layer(z, carry, last):
            norm, curv = carry
            for y in range(rows):
                b = z * rows + y
                here, cell = grad[b], model[b]
                square = here * here
                norm = norm + square
                dx = pltpu.roll(here, 127, 1) - here
                part = conduct(cell, row_of(face_small, b)) * square
                part = part + conduct(
                    pltpu.roll(cell, 127, 1) - cell, row_of(face_x, b)
                ) * (dx * dx)
                if not last:
                    dz = grad[b + rows] - here
                    part = part + conduct(model[b + rows] - cell, row_of(face_z, b)) * (dz * dz)
                if y < rows - 1:
                    dy = grad[b + 1] - here
                    part = part + conduct(model[b + 1] - cell, row_of(face_y, b)) * (dy * dy)
                curv = curv + part
            return norm, curv

        zero = jnp.zeros((8, 128), F32)
        carry = lax.fori_loop(
            0, layers - 1, functools.partial(one_layer, last=False), (zero, zero)
        )
        return one_layer(layers - 1, carry, True)

    def shared_faces(norm, curv, after, base):
        await_grad_halo(recv_sem, base, after)
        for y in range(rows):
            b = (layers - 1) * rows + y
            dz = grad_z[after, y].astype(F32) - grad[b]
            curv = curv + conduct(halo_z[1, y] - model[b], row_of(face_z, b)) * (dz * dz)
        for z in range(layers):
            b = z * rows + rows - 1
            dy = grad_y[after, z].astype(F32) - grad[b]
            curv = curv + conduct(halo_y[1, z] - model[b], row_of(face_y, b)) * (dy * dy)
        return (
            jnp.sum(norm, axis=1, keepdims=True),
            jnp.sum(curv * scale, axis=1, keepdims=True),
        )

    def forward(t, number):
        for e in range(width):
            picked[t, :, e * 128 : (e + 1) * 128] = came[number][
                slot_of[0, t * width + e]
            ].astype(F32)
        return jnp.dot(picked[t].astype(BF16), sens_t[t], preferred_element_type=F32)

    def backward(t, weighted):
        chunk = 1024
        for c in range(width * 128 // chunk):
            made = lax.dot_general(
                weighted,
                sens[t, :, c * chunk : (c + 1) * chunk],
                (((1,), (0,)), ((), ())),
                preferred_element_type=F32,
            )
            for j in range(chunk // 128):
                entry = t * width + c * (chunk // 128) + j
                product[entry] = made[:, j * 128 : (j + 1) * 128]

    def mask_of(t):
        slot = lax.broadcasted_iota(jnp.int32, (1, slots), 1)
        return jnp.where(slot < counts[t], 1.0, 0.0)

    def weight_of(t):
        weight = data_weight[pl.ds(t, 1), :]
        return mask_of(t) * (weight * weight)

    def scatter(number):
        def widen(d, c):
            spread[pl.ds(pl.multiple_of(d * 8, 8), 8), :] = came[number][d].astype(F32)
            return c

        lax.fori_loop(0, 2 * owners, widen, 0, unroll=8)
        table = one_hot[...]
        for s in range(0, 8, 2):
            pair = []
            for sample_row in (s, s + 1):
                first = spread[pl.ds(sample_row, owners, stride=16), :]
                second = spread[pl.ds(8 + sample_row, owners, stride=16), :]
                pair.append(jnp.concatenate([first, second], axis=0).astype(BF16))
            made = jnp.dot(
                table, jnp.concatenate(pair, axis=1), preferred_element_type=F32
            )
            sums[pl.ds(s, cells, stride=8), :] = made[:, :128]
            sums[pl.ds(s + 1, cells, stride=8), :] = made[:, 128:]

    def make_gradient(step):
        def one(b, c):
            total = row_of(is_active, b) * sums[pl.ds(pl.multiple_of(b * 8, 8), 8), :]
            grad[b] = reg_part[b] + total if step is None else reg_part[b] - step * total
            return c

        lax.fori_loop(0, cells, one, 0, unroll=8)

    def sum_start(mine, number):
        sum_mine[number, 0] = mine
        sum_a[number, survey] = mine

        def send(i, c):
            to = (survey + i) % surveys
            remote(
                sum_mine.at[number, 0], sum_a.at[number, survey], 6 + 2 * number, (region, to)
            ).start()
            return c

        lax.fori_loop(1, surveys, send, 0)

    def sum_middle(number):
        await_bytes(sum_a.at[number, pl.ds(0, surveys - 1)], recv_sem.at[6 + 2 * number])
        part = sum_a[number, 0]
        for i in range(1, surveys):
            part = part + sum_a[number, i]
        sum_mine[number, 1] = part
        sum_b[number, region] = part

        def send(i, c):
            to = (region + i) % regions
            remote(
                sum_mine.at[number, 1], sum_b.at[number, region], 7 + 2 * number, (to, survey)
            ).start()
            return c

        lax.fori_loop(1, regions, send, 0)

    def sum_end(number):
        await_bytes(sum_b.at[number, pl.ds(0, regions - 1)], recv_sem.at[7 + 2 * number])
        whole = sum_b[number, 0]
        for i in range(1, regions):
            whole = whole + sum_b[number, i]
        norm = jnp.sum(jnp.where(lane == 0, whole, 0.0), axis=1, keepdims=True)
        curv = jnp.sum(jnp.where(lane == 1, whole, 0.0), axis=1, keepdims=True)
        return norm / curv

    def my_sums(norm, reg_curv, data_curv):
        return jnp.where(lane == 0, norm, jnp.where(lane == 1, reg_curv + data_curv, 0.0))

    await_halo(halo_z, halo_y, 10)
    regularize(False)
    turn(2)
    turn(3)
    load_observed.wait()
    load_weight.wait()

    await_round(1)
    for t in range(tiles):
        gap = forward(t, 1) - observed[t]
        residual[t] = gap
        backward(t, (weight_of(t) * gap).astype(BF16))
    give_back(2)
    await_round(2)
    scatter(2)
    make_gradient(None)
    fetch(grad, 3)
    send_grad_halo(14, 0, 0)
    inner = curvature()

    await_round(3)
    send_grad_halo(16, 1, 1)
    data_curv = jnp.zeros((8, 1), F32)
    for t in range(tiles):
        made = forward(t, 3)
        step_pred[t] = made
        data_curv = data_curv + jnp.sum(weight_of(t) * made * made, axis=1, keepdims=True)
    norm, reg_curv = shared_faces(*inner, 0, 14)
    sum_start(my_sums(norm, reg_curv, data_curv), 0)
    for t in range(tiles):
        backward(t, (weight_of(t) * step_pred[t]).astype(BF16))
    give_back(4, lambda: sum_middle(0))
    step = sum_end(0)
    sent_halo(model, 10)
    step_row = jnp.broadcast_to(step, (8, 128))

    def move(b, c):
        model[b] = model[b] - step_row * grad[b]
        return c

    lax.fori_loop(0, cells, move, 0, unroll=8)
    await_grad_halo(recv_sem, 16, 1)
    for side in range(2):
        for y in range(rows):
            halo_z[side, y] = halo_z[side, y] - step_row * grad_z[1 - side, y].astype(F32)
        for z in range(layers):
            halo_y[side, z] = halo_y[side, z] - step_row * grad_y[1 - side, z].astype(F32)
    save_model = load(model, model_out, 12)
    regularize(True)
    for t in range(tiles):
        residual[t] = residual[t] - step * step_pred[t]

    await_round(4)
    scatter(4)
    make_gradient(step_row)
    fetch(grad, 5)
    send_grad_halo(18, 0, 2)
    save_grad = load(grad, grad_out, 13)
    inner = curvature()

    await_round(5)
    data_curv = jnp.zeros((8, 1), F32)
    for t in range(tiles):
        made = forward(t, 5)
        step_pred[t] = made
        data_curv = data_curv + jnp.sum(weight_of(t) * made * made, axis=1, keepdims=True)
    norm, reg_curv = shared_faces(*inner, 2, 18)
    sum_start(my_sums(norm, reg_curv, data_curv), 1)
    sum_middle(1)
    step = sum_end(1)
    step_out[...] = jnp.broadcast_to(step, (8, 128))
    for t in range(tiles):
        weight = mask_of(t) * data_weight[pl.ds(t, 1), :]
        misfit_out[t] = weight * (residual[t] - step * step_pred[t])

    await_bytes(ask.at[pl.ds(0, owners - 1)], send_sem.at[0])
    for number in range(4, 6):
        await_bytes(sent[number].at[pl.ds(0, 2 * owners - 2)], send_sem.at[number])
    for number in range(2):
        await_bytes(sum_a.at[number, pl.ds(0, surveys - 1)], send_sem.at[6 + 2 * number])
        await_bytes(sum_b.at[number, pl.ds(0, regions - 1)], send_sem.at[7 + 2 * number])
    for stage in range(3):
        await_grad_halo(send_sem, 14 + 2 * stage, stage)
    save_model.wait()
    save_grad.wait()


def finish(moved, gradient, step, misfit, final_out, misfit_out, made, sem):
    parts = made.shape[0]
    size = made.shape[1]
    copy_misfit = pltpu.make_async_copy(misfit, misfit_out, sem.at[parts])
    copy_misfit.start()
    copies = []
    for i in range(parts):
        for b in range(size):
            made[i, b] = moved[i * size + b] - step[...] * gradient[i * size + b]
        copies.append(
            pltpu.make_async_copy(made.at[i], final_out.at[pl.ds(i * size, size)], sem.at[i])
        )
        copies[-1].start()
    for copy in copies:
        copy.wait()
    copy_misfit.wait()


def shards(
    regions,
    surveys,
    sensitivity,
    observed,
    data_weight,
    data_counts,
    tile_bricks,
    start_model,
    active_cells,
    face_links,
    reg_weight,
):
    layers, rows, samples, across = start_model.shape
    tiles, width = tile_bricks.shape
    slots = sensitivity.shape[1]
    owners, cells = regions * surveys, layers * rows
    entries = tiles * width

    field = jax.ShapeDtypeStruct((cells, samples, across), F32)
    field_scratch = pltpu.VMEM(field.shape, F32)
    blocks = pltpu.VMEM((2 * owners, samples, across), BF16)
    data_scratch = pltpu.VMEM((tiles, samples, slots), F32)
    plane = pltpu.VMEM((cells, across), F32)
    vmem = pl.BlockSpec(memory_space=pltpu.VMEM)
    smem = pl.BlockSpec(memory_space=pltpu.SMEM)
    anywhere = pl.BlockSpec(memory_space=pl.ANY)
    in_hbm = pl.BlockSpec(memory_space=pltpu.HBM)
    moved, gradient, step, misfit = pl.pallas_call(
        functools.partial(kernel, (regions, surveys, layers, rows, tiles, width, slots)),
        name="inversion",
        out_shape=(
            field,
            field,
            jax.ShapeDtypeStruct((samples, across), F32),
            jax.ShapeDtypeStruct((tiles, samples, slots), F32),
        ),
        in_specs=[smem] * 2 + [vmem] + [in_hbm] * 6,
        out_specs=(anywhere, anywhere, vmem, vmem),
        scratch_shapes=[
            pltpu.VMEM(sensitivity.shape, BF16),
            pltpu.VMEM((tiles, width * across, slots), BF16),
            field_scratch,
            field_scratch,
            pltpu.VMEM((cells * samples, across), F32),
            field_scratch,
            pltpu.VMEM(observed.shape, F32),
            pltpu.VMEM(data_weight.shape, F32),
            pltpu.VMEM((cells, across), jnp.int32),
            pltpu.VMEM((cells, across), jnp.int32),
            *[plane] * 5,
            pltpu.VMEM((rows, across), F32),
            pltpu.VMEM((layers * 8, across), F32),
            pltpu.VMEM((rows, 8, 128), F32),
            pltpu.VMEM((owners, 1, 128), jnp.int32),
            pltpu.VMEM((owners, 1, 128), jnp.int32),
            pltpu.VMEM((2, owners), jnp.int32),
            pltpu.SMEM((2, owners), jnp.int32),
            pltpu.VMEM((1, entries), jnp.int32),
            pltpu.VMEM((2, owners), jnp.int32),
            pltpu.SMEM((1, entries), jnp.int32),
            pltpu.SMEM((2, owners), jnp.int32),
            pltpu.VMEM((tiles, samples, width * 128), F32),
            pltpu.VMEM((entries, samples, across), F32),
            data_scratch,
            data_scratch,
            *[blocks] * 4,
            pltpu.VMEM((owners * 16, 128), F32),
            pltpu.VMEM((cells, 2 * owners), BF16),
            pltpu.VMEM((2, layers, 8, 128), F32),
            pltpu.VMEM((3, rows, 8, 128), BF16),
            pltpu.VMEM((3, layers, 8, 128), BF16),
            pltpu.VMEM((2, rows, 8, 128), F32),
            pltpu.VMEM((2, layers, 8, 128), F32),
            pltpu.VMEM((3, rows, 8, 128), BF16),
            pltpu.VMEM((3, layers, 8, 128), BF16),
            pltpu.VMEM((2, 2, 8, 128), F32),
            pltpu.VMEM((2, surveys, 8, 128), F32),
            pltpu.VMEM((2, regions, 8, 128), F32),
            pltpu.SemaphoreType.DMA((14,)),
            pltpu.SemaphoreType.DMA((20,)),
            pltpu.SemaphoreType.DMA((20,)),
        ],
        compiler_params=pltpu.CompilerParams(
            collective_id=0, has_side_effects=True, vmem_limit_bytes=97 << 19
        ),
    )(
        *(
            pltpu.with_memory_space_constraint(x, pltpu.HBM)
            for x in (
                data_counts,
                reg_weight,
                tile_bricks,
                observed,
                data_weight,
                active_cells.reshape(cells, across),
                face_links.reshape(cells, across),
                start_model.reshape(cells, samples, across),
                sensitivity,
            )
        )
    )
    parts = 8
    final, misfit = pl.pallas_call(
        finish,
        name="finish",
        out_shape=(field, jax.ShapeDtypeStruct(misfit.shape, F32)),
        in_specs=[vmem] * 4,
        out_specs=(in_hbm, in_hbm),
        scratch_shapes=[
            pltpu.VMEM((parts, cells // parts, samples, across), F32),
            pltpu.SemaphoreType.DMA((parts + 1,)),
        ],
        compiler_params=pltpu.CompilerParams(vmem_limit_bytes=8 << 20),
    )(moved, gradient, step, misfit)
    return final.reshape(start_model.shape), misfit


def solution(mesh):
    return jax.shard_map(
        functools.partial(shards, mesh.shape["region"], mesh.shape["survey"]),
        mesh=mesh,
        in_specs=(
            P(("region", "survey"), None, None),
            P(("region", "survey"), None, None),
            P(("region", "survey"), None),
            P(("region", "survey")),
            P(("region", "survey"), None),
            P("region", "survey", None, None),
            P("region", "survey", None),
            P("region", "survey", None),
            P(),
        ),
        out_specs=(P("region", "survey", None, None), P(("region", "survey"), None, None)),
        check_vma=False,
    )
```
